32 devices in a mesh: radial: 8 (over y, x, core), mode: 4 (over z).
Axes of the slice: x: 2, y: 2, z: 4, core: 2. Of those that a mesh axis runs over, the one named last changes fastest.
Arguments:
- scalar_field: float32 [256, 64, 2, 384], P('radial', 'mode'), may hold values from -48 to 48
- radial_flow: float32 [256, 64, 2, 384], P('radial', 'mode'), may hold values from -6 to 6
- legendre: bfloat16 [64, 384, 768], P('mode'), may hold values from -0.3125 to 0.3125
- diffusivity: float32 [256], P('radial'), may hold values from 1000 to 100000
Outputs:
- field_new: float32 [256, 64, 2, 384], P('radial', 'mode')
The draws below stay inside these ranges and needn't reach their ends.
All inputs are finite; a program needn't handle non-finite values.
Results may differ from the reference program's by a relative error of at most 0.0071.
Values may be sent and summed in bfloat16 or wider, within the bound.
A program may use at most 128 MiB of HBM per device.

```python
import math
import jax
import jax.numpy as jnp
from jax import lax

DEG = 384
NLAT = 768
NLON = 1536
NR = 256
ORDERS = 64
ROFF = 137


def shard_levels(key, dims, cuts, smallest, high):
    gain = 1.0
    for dim, parts in cuts:
        draws = jax.random.uniform(jax.random.fold_in(jax.random.fold_in(key, 6), dim), (parts,), jnp.float32, smallest / len(cuts), high / len(cuts))
        gain = gain * jnp.repeat(jnp.exp(draws), dims[dim] // parts).reshape((-1,) + (1,) * (len(dims) - 1 - dim))
    return gain


def normal_values(stream_key, dims, width, reach, split=(), held_as=jnp.bfloat16):
    drawn = jax.random.normal(stream_key, dims, jnp.float32) * width
    if len(split) > 0:
        drawn = shard_levels(stream_key, dims, split, -0.22, 0.18) * drawn
    return jnp.clip(drawn, min=-reach, max=reach).astype(held_as)


def setup_inputs(seed: int = 0) -> dict:
    seeds = jax.random.split(jax.random.key(seed), 5)
    return {
        "scalar_field": normal_values(seeds[0], (NR, ORDERS, 2, DEG), 8.0, 48.0, ((0, 8), (1, 4)), jnp.float32),
        "radial_flow": normal_values(seeds[1], (NR, ORDERS, 2, DEG), 1.0, 6.0, ((0, 8), (1, 4)), jnp.float32),
        "legendre": normal_values(seeds[2], (ORDERS, DEG, NLAT), DEG ** -0.5, 0.3125, ((0, 4),)),
        "diffusivity": jnp.clip(jnp.exp(math.log(100000.0) - 4.6051702 * jax.random.uniform(seeds[3], (NR,), jnp.float32) ** shard_levels(seeds[3], (NR,), ((0, 8),), -0.2, 0.2)), 1000.0, 100000.0),
    }


def longitude_tables(orders, points):
    order_ids = jnp.arange(orders, dtype=jnp.int32)
    point_ids = jnp.arange(points, dtype=jnp.int32)
    phase = order_ids[:, None] * point_ids[None, :] % points
    angle = phase.astype(jnp.float32) * (2.0 * math.pi / points)
    cosine = jnp.cos(angle)
    sine_part = jnp.sin(angle)
    paired = jnp.stack([cosine, -sine_part], axis=1)
    synth_table = (paired / math.sqrt(orders)).astype(jnp.bfloat16)
    analysis_table = (paired * math.sqrt(2.0 / points)).astype(jnp.bfloat16)
    return (synth_table, analysis_table)

def rounded(values):
    return lax.optimization_barrier(values.astype(jnp.bfloat16)).astype(jnp.float32)

def tridiagonal_solve(right_side, diffusivity):
    degree = jnp.arange(ORDERS, dtype=jnp.float32)[:, None] + jnp.arange(DEG, dtype=jnp.float32)[None, :]
    angular = degree * (degree + 1.0)
    shell_ids = jnp.arange(NR, dtype=jnp.int32)

    def forward(carry, inputs):
        ratio_prev, value_prev = carry
        kappa_shell, source, shell_index = inputs
        lower = jnp.where(shell_index > 0, -kappa_shell, 0.0)
        upper = jnp.where(shell_index < NR - 1, -kappa_shell, 0.0)
        radius = (ROFF + shell_index).astype(jnp.float32)
        diagonal = 1.0 + 2.0 * kappa_shell + kappa_shell * angular / (radius * radius)
        pivot = diagonal - lower * ratio_prev
        ratio_now = upper / pivot
        value_now = (source - lower * value_prev) / pivot[:, None, :]
        return ((ratio_now, value_now), (ratio_now, value_now))
    blank_ratio = jnp.zeros((ORDERS, DEG), jnp.float32)
    blank_value = jnp.zeros((ORDERS, 2, DEG), jnp.float32)
    _, (ratios, values) = lax.scan(forward, (blank_ratio, blank_value), (diffusivity, right_side, shell_ids))

    def backward(beyond, inputs):
        ratio_now, value_now = inputs
        solved = value_now - ratio_now[:, None, :] * beyond
        return (solved, solved)
    _, solution = lax.scan(backward, blank_value, (ratios, values), reverse=True)
    return solution

def reference(scalar_field, radial_flow, legendre, diffusivity):
    synth_table, analysis_table = longitude_tables(ORDERS, NLON)
    synth_wide = synth_table.astype(jnp.float32)
    analysis_wide = analysis_table.astype(jnp.float32)
    legendre_wide = legendre.astype(jnp.float32)

    def shell_forcing(shell_pair):
        field_shell, flow_shell = shell_pair
        field_lat = rounded(jnp.einsum('mcj,mjt->mct', rounded(field_shell), legendre_wide))
        flow_lat = rounded(jnp.einsum('mcj,mjt->mct', rounded(flow_shell), legendre_wide))
        field_grid = jnp.einsum('mct,mcp->tp', field_lat, synth_wide)
        flow_grid = jnp.einsum('mct,mcp->tp', flow_lat, synth_wide)
        product = rounded(field_grid * flow_grid)
        product_modes = rounded(jnp.einsum('tp,mcp->mct', product, analysis_wide))
        return jnp.einsum('mct,mjt->mcj', product_modes, legendre_wide)
    forcing = lax.map(shell_forcing, (scalar_field, radial_flow))
    right_side = scalar_field + forcing
    return tridiagonal_solve(right_side, diffusivity)
```

```python
import functools
import math

import jax
import jax.numpy as jnp
import numpy as np
from jax import lax
from jax.experimental import pallas as pl
from jax.experimental.pallas import tpu as pltpu
from jax.sharding import PartitionSpec as P

NLON = 1536
VMEM_LIMIT = 60 * 1024 * 1024


def params(**more):
    return pltpu.CompilerParams(vmem_limit_bytes=VMEM_LIMIT, **more)


def grid_points(orders):
    needed = 3 * (orders - 1) + 1
    return next(q for q in range(128, NLON + 1, 128) if q >= needed and NLON % q == 0)


def longitude_tables(orders):
    points = grid_points(orders)
    stride = NLON // points
    phase = np.arange(orders)[:, None] * (np.arange(points) * stride)[None, :] % NLON
    angle = phase.astype(np.float32) * np.float32(2.0 * math.pi / NLON)
    paired = np.stack([np.cos(angle), -np.sin(angle)], axis=1).reshape(2 * orders, points)
    synth = (paired / np.float32(math.sqrt(orders))).astype(jnp.bfloat16)
    analysis = (paired * np.float32(math.sqrt(2.0 / NLON))).astype(jnp.bfloat16)
    return jnp.asarray(synth.T), jnp.asarray(analysis), float(stride)


def to_latitudes(parts, field_ref, flow_ref, table_ref, out_ref, rows_ref):
    order = pl.program_id(0)
    shells = field_ref.shape[0]
    lanes = rows_ref.shape[0]
    count = 4 * shells
    stacked = jnp.concatenate(
        [ref[:, 0, half, :] for half in range(2) for ref in (field_ref, flow_ref)], axis=0
    ).astype(jnp.bfloat16)
    lat = jnp.dot(stacked, table_ref[0], preferred_element_type=jnp.float32)
    base = pl.multiple_of(order * count, count)
    for lane in range(lanes):
        rows_ref[lane, pl.ds(base, count), :] = lat[:, lane * 128 : (lane + 1) * 128]

    @pl.when(order == pl.num_programs(0) - 1)
    def _():
        mine = shells // parts
        modes = rows_ref.shape[1] // (2 * shells)
        for part in range(parts):
            for which in range(2):
                for shell in range(mine):
                    start = which * shells + part * mine + shell
                    for lane in range(lanes):
                        picked = rows_ref[lane, pl.ds(start, modes, stride=2 * shells), :]
                        out_ref[part, which, shell, :, lane * 128 : (lane + 1) * 128] = (
                            picked.astype(jnp.bfloat16)
                        )


def through_grid(scale, lat_ref, synth_ref, analysis_ref, out_ref):
    parts, _, _, modes, _ = lat_ref.shape
    grids = []
    for which in range(2):
        lat = jnp.concatenate([lat_ref[part, which, 0] for part in range(parts)], axis=0)
        grids.append(jnp.dot(synth_ref[...], lat, preferred_element_type=jnp.float32))
    product = (grids[0] * grids[1]).astype(jnp.bfloat16)
    back = jnp.dot(analysis_ref[...], product, preferred_element_type=jnp.float32) * scale
    for part in range(parts):
        out_ref[part, 0] = back[part * modes : (part + 1) * modes].astype(jnp.bfloat16)


def eliminate(
    nr_total, where_ref, kappa_ref, back_ref, table_ref, field_ref,
    alpha_ref, beta_ref, gamma_ref, edge_ref, wide_ref, right_ref,
):
    order = pl.program_id(0)
    shells, modes, _ = back_ref.shape
    ord_dev = modes // 2
    degrees = field_ref.shape[3]
    lanes = wide_ref.shape[0]
    blocks = right_ref.shape[0]

    @pl.when(order == 0)
    def _():
        for shell in range(shells):
            for lane in range(lanes):
                wide_ref[lane, shell * modes : (shell + 1) * modes, :] = back_ref[
                    shell, :, lane * 128 : (lane + 1) * 128
                ].astype(jnp.float32)

    picked = jnp.concatenate(
        [
            jnp.concatenate(
                [
                    wide_ref[lane, pl.ds(2 * order + half, shells, stride=modes), :].astype(jnp.bfloat16)
                    for lane in range(lanes)
                ],
                axis=1,
            )
            for half in range(2)
        ],
        axis=0,
    )
    forcing = lax.dot_general(
        picked, table_ref[0], (((1,), (1,)), ((), ())), preferred_element_type=jnp.float32
    )
    for half in range(2):
        right = field_ref[:, 0, half, :] + forcing[half * shells : (half + 1) * shells]
        for block in range(blocks):
            right_ref[block, pl.ds(half * ord_dev + order, shells, stride=modes), :] = right[
                :, block * 128 : (block + 1) * 128
            ]

    @pl.when(order == pl.num_programs(0) - 1)
    def _():
        first = where_ref[0] * shells
        first_order = where_ref[1] * ord_dev
        offset = nr_total * 7 // 13
        for block in range(blocks):
            at = slice(block * 128, (block + 1) * 128)
            degree = (
                first_order
                + block * 128
                + lax.broadcasted_iota(jnp.int32, (ord_dev, 128), 0)
                + lax.broadcasted_iota(jnp.int32, (ord_dev, 128), 1)
            ).astype(jnp.float32)
            angular = degree * (degree + 1.0)

            def forward(shell, carry):
                ratio, value0, value1, pull = carry
                index = first + shell
                kappa = kappa_ref[shell]
                lower = jnp.where(index > 0, -kappa, 0.0)
                upper = jnp.where(index < nr_total - 1, -kappa, 0.0)
                radius = jnp.full((ord_dev, 128), offset + index, jnp.int32).astype(jnp.float32)
                diagonal = 1.0 + 2.0 * kappa + kappa * angular / (radius * radius)
                inverse = 1.0 / (diagonal - lower * ratio)
                start = pl.multiple_of(shell * modes, modes)
                ratio = upper * inverse
                value0 = (right_ref[block, pl.ds(start, ord_dev), :] - lower * value0) * inverse
                value1 = (
                    right_ref[block, pl.ds(start + ord_dev, ord_dev), :] - lower * value1
                ) * inverse
                pull = -lower * pull * inverse
                alpha_ref[shell, :ord_dev, at] = value0
                alpha_ref[shell, ord_dev:, at] = value1
                beta_ref[shell, :, at] = pull
                gamma_ref[shell, :, at] = ratio
                return ratio, value0, value1, pull

            blank = jnp.zeros((ord_dev, 128), jnp.float32)
            unity = jnp.ones((ord_dev, 128), jnp.float32)
            lax.fori_loop(0, shells, forward, (blank, blank, blank, unity), unroll=4)

            def backward(step, carry):
                alpha0, alpha1, beta, gamma = carry
                shell = shells - 1 - step
                ratio = gamma_ref[shell, :, at]
                alpha0 = alpha_ref[shell, :ord_dev, at] - ratio * alpha0
                alpha1 = alpha_ref[shell, ord_dev:, at] - ratio * alpha1
                beta = beta_ref[shell, :, at] - ratio * beta
                gamma = -ratio * gamma
                alpha_ref[shell, :ord_dev, at] = alpha0
                alpha_ref[shell, ord_dev:, at] = alpha1
                beta_ref[shell, :, at] = beta
                gamma_ref[shell, :, at] = gamma
                return alpha0, alpha1, beta, gamma

            lax.fori_loop(0, shells, backward, (blank, blank, blank, unity), unroll=4)
            for side, shell in enumerate((0, shells - 1)):
                edge_ref[4 * side, :, at] = alpha_ref[shell, :ord_dev, at]
                edge_ref[4 * side + 1, :, at] = alpha_ref[shell, ord_dev:, at]
                edge_ref[4 * side + 2, :, at] = beta_ref[shell, :, at]
                edge_ref[4 * side + 3, :, at] = gamma_ref[shell, :, at]


def finish(where_ref, edges_ref, alpha_ref, beta_ref, gamma_ref, out_ref):
    count = edges_ref.shape[0]
    shells, modes, degrees = alpha_ref.shape
    ord_dev = modes // 2
    mine = where_ref[0]
    for block in range(degrees // 128):
        at = slice(block * 128, (block + 1) * 128)
        blank = jnp.zeros((ord_dev, 128), jnp.float32)
        known = [blank, blank]
        slope = blank
        lefts, firsts = [], []
        for device in range(count):
            head = [edges_ref[device, k, :, at] for k in range(4)]
            tail = [edges_ref[device, 4 + k, :, at] for k in range(4)]
            lefts.append((known, slope))
            inverse = 1.0 / (1.0 - head[2] * slope)
            const = [(head[c] + head[2] * known[c]) * inverse for c in range(2)]
            gain = head[3] * inverse
            firsts.append((const, gain))
            known = [tail[c] + tail[2] * (known[c] + slope * const[c]) for c in range(2)]
            slope = tail[3] + tail[2] * slope * gain
        beyond = [blank, blank]
        before = [blank, blank]
        after = [blank, blank]
        for device in reversed(range(count)):
            const, gain = firsts[device]
            left, tilt = lefts[device]
            here = mine == device
            start = [const[c] + gain * beyond[c] for c in range(2)]
            before = [jnp.where(here, left[c] + tilt * start[c], before[c]) for c in range(2)]
            after = [jnp.where(here, beyond[c], after[c]) for c in range(2)]
            beyond = start

        def emit(shell, carry):
            beta, gamma = beta_ref[shell, :, at], gamma_ref[shell, :, at]
            for half in range(2):
                out_ref[shell, :, half, at] = (
                    alpha_ref[shell, half * ord_dev : (half + 1) * ord_dev, at]
                    + beta * before[half]
                    + gamma * after[half]
                )
            return carry

        lax.fori_loop(0, shells, emit, 0, unroll=4)


def on_device(scalar_field, radial_flow, legendre, diffusivity):
    shells, ord_dev, _, degrees = scalar_field.shape
    lats = legendre.shape[2]
    parts, rings = lax.axis_size("mode"), lax.axis_size("radial")
    orders = ord_dev * parts
    modes = 2 * ord_dev
    mine = shells // parts
    synth, analysis, scale = longitude_tables(orders)
    points = synth.shape[0]
    where = jnp.stack([lax.axis_index("radial"), lax.axis_index("mode")]).astype(jnp.int32)

    spectral = pl.BlockSpec((shells, 1, 2, degrees), lambda m: (0, m, 0, 0))
    table = pl.BlockSpec((1, degrees, lats), lambda m: (m, 0, 0))
    smem = pl.BlockSpec(memory_space=pltpu.SMEM)

    def whole(*shape):
        return pl.BlockSpec(shape, lambda *_: (0,) * len(shape))

    lat = pl.pallas_call(
        functools.partial(to_latitudes, parts),
        grid=(ord_dev,),
        in_specs=[spectral, spectral, table],
        out_specs=whole(parts, 2, mine, modes, lats),
        out_shape=jax.ShapeDtypeStruct((parts, 2, mine, modes, lats), jnp.bfloat16),
        scratch_shapes=[pltpu.VMEM((lats // 128, 4 * shells * ord_dev, 128), jnp.float32)],
        compiler_params=params(),
        name="to_latitudes",
    )(scalar_field, radial_flow, legendre)
    lat = lax.all_to_all(lat, "mode", split_axis=0, concat_axis=0, tiled=True)
    back = pl.pallas_call(
        functools.partial(through_grid, scale),
        grid=(mine,),
        in_specs=[
            pl.BlockSpec((parts, 2, 1, modes, lats), lambda r: (0, 0, r, 0, 0)),
            whole(points, 2 * orders),
            whole(2 * orders, points),
        ],
        out_specs=pl.BlockSpec((parts, 1, modes, lats), lambda r: (0, r, 0, 0)),
        out_shape=jax.ShapeDtypeStruct((parts, mine, modes, lats), jnp.bfloat16),
        compiler_params=params(),
        name="through_grid",
    )(lat, synth, analysis)
    back = lax.all_to_all(back, "mode", split_axis=0, concat_axis=0, tiled=True)
    back = back.reshape(shells, modes, lats)
    f32 = jnp.float32
    alpha, beta, gamma, edge = pl.pallas_call(
        functools.partial(eliminate, shells * rings),
        grid=(ord_dev,),
        in_specs=[smem, smem, whole(shells, modes, lats), table, spectral],
        out_specs=[
            whole(shells, modes, degrees),
            whole(shells, ord_dev, degrees),
            whole(shells, ord_dev, degrees),
            whole(8, ord_dev, degrees),
        ],
        out_shape=[
            jax.ShapeDtypeStruct((shells, modes, degrees), f32),
            jax.ShapeDtypeStruct((shells, ord_dev, degrees), f32),
            jax.ShapeDtypeStruct((shells, ord_dev, degrees), f32),
            jax.ShapeDtypeStruct((8, ord_dev, degrees), f32),
        ],
        scratch_shapes=[
            pltpu.VMEM((lats // 128, shells * modes, 128), f32),
            pltpu.VMEM((degrees // 128, shells * modes, 128), f32),
        ],
        compiler_params=params(),
        name="eliminate",
    )(where, diffusivity, back, legendre, scalar_field)
    edges = lax.all_gather(edge, "radial")
    return pl.pallas_call(
        finish,
        in_specs=[smem] + [pl.BlockSpec(memory_space=pltpu.VMEM)] * 4,
        out_specs=pl.BlockSpec(memory_space=pltpu.VMEM),
        out_shape=jax.ShapeDtypeStruct(scalar_field.shape, f32),
        compiler_params=params(),
        name="finish",
    )(where, edges, alpha, beta, gamma)


def solution(mesh):
    return jax.shard_map(
        on_device,
        mesh=mesh,
        in_specs=(
            P("radial", "mode", None, None),
            P("radial", "mode", None, None),
            P("mode", None, None),
            P("radial"),
        ),
        out_specs=P("radial", "mode", None, None),
        check_vma=False,
    )
```

```python
import functools
import math

import jax
import jax.numpy as jnp
import numpy as np
from jax import lax
from jax.experimental import pallas as pl
from jax.experimental.pallas import tpu as pltpu
from jax.sharding import PartitionSpec as P

NLON = 1536
VMEM_LIMIT = 60 * 1024 * 1024


def params(**more):
    return pltpu.CompilerParams(vmem_limit_bytes=VMEM_LIMIT, **more)


def grid_points(orders):
    needed = 3 * (orders - 1) + 1
    return next(q for q in range(128, NLON + 1, 128) if q >= needed and NLON % q == 0)


def longitude_tables(orders):
    points = grid_points(orders)
    stride = NLON // points
    phase = np.arange(orders)[:, None] * (np.arange(points) * stride)[None, :] % NLON
    angle = phase.astype(np.float32) * np.float32(2.0 * math.pi / NLON)
    paired = np.stack([np.cos(angle), -np.sin(angle)], axis=1).reshape(2 * orders, points)
    synth = (paired / np.float32(math.sqrt(orders))).astype(jnp.bfloat16)
    analysis = (paired * np.float32(math.sqrt(2.0 / NLON))).astype(jnp.bfloat16)
    return jnp.asarray(synth.T), jnp.asarray(analysis), float(stride)


def whole_step(
    chunks, scale, kappa_ref, table_hbm, field_ref, flow_ref, synth_ref, analysis_ref, out_ref,
    table_ref, spectral_ref, rows_ref, send_ref, recv_ref, back_send_ref, back_recv_ref,
    wide_ref, sum_ref, right_ref, alpha_ref, beta_ref, gamma_ref, edge_ref, edges_ref,
    table_sem, send_sem, recv_sem, back_send_sem, back_recv_sem, edge_send_sem, edge_recv_sem,
):
    shells, ord_dev, _, degrees = field_ref.shape
    modes = 2 * ord_dev
    parts, rings = lax.axis_size("mode"), lax.axis_size("radial")
    me, ring = lax.axis_index("mode"), lax.axis_index("radial")
    mine = shells // parts
    count = 4 * shells
    width = table_ref.shape[3]
    lanes, blocks = width // 128, degrees // 128
    nr_total = shells * rings

    def table_copy(chunk):
        return pltpu.make_async_copy(
            table_hbm.at[:, :, pl.ds(chunk * width, width)], table_ref.at[chunk], table_sem.at[chunk]
        )

    for chunk in range(chunks):
        table_copy(chunk).start()

    barrier = pltpu.get_barrier_semaphore()
    for hop in range(1, parts):
        pl.semaphore_signal(
            barrier, inc=1, device_id={"mode": lax.rem(me + hop, parts)},
            device_id_type=pl.DeviceIdType.MESH,
        )
    for hop in range(1, rings):
        pl.semaphore_signal(
            barrier, inc=1, device_id={"radial": lax.rem(ring + hop, rings)},
            device_id_type=pl.DeviceIdType.MESH,
        )

    def exchange(axis, hop, source, target, send, receive):
        here, size = (me, parts) if axis == "mode" else (ring, rings)
        return pltpu.make_async_remote_copy(
            src_ref=source, dst_ref=target, send_sem=send, recv_sem=receive,
            device_id={axis: lax.rem(here + hop, size)}, device_id_type=pl.DeviceIdType.MESH,
        )

    def lat_copy(chunk, hop, slot):
        to = lax.rem(me + hop, parts)
        return exchange(
            "mode", hop, send_ref.at[chunk, to], recv_ref.at[chunk, slot],
            send_sem.at[chunk, hop - 1], recv_sem.at[chunk, hop - 1],
        )

    def back_copy(chunk, hop, slot):
        to = lax.rem(me + hop, parts)
        return exchange(
            "mode", hop, back_send_ref.at[chunk, to], back_recv_ref.at[chunk, slot],
            back_send_sem.at[chunk, hop - 1], back_recv_sem.at[chunk, hop - 1],
        )

    def edge_copy(hop, slot):
        return exchange(
            "radial", hop, edge_ref, edges_ref.at[slot],
            edge_send_sem.at[hop - 1], edge_recv_sem.at[hop - 1],
        )

    def stack(order, carry):
        spectral_ref[order] = jnp.concatenate(
            [ref[:, order, half, :] for half in range(2) for ref in (field_ref, flow_ref)], axis=0
        ).astype(jnp.bfloat16)
        return carry

    lax.fori_loop(0, ord_dev, stack, 0, unroll=2)

    for chunk in range(chunks):
        table_copy(chunk).wait()

        def transform(order, carry):
            lat = jnp.dot(
                spectral_ref[order], table_ref[chunk, order], preferred_element_type=jnp.float32
            )
            base = pl.multiple_of(order * count, count)
            for lane in range(lanes):
                rows_ref[lane, pl.ds(base, count), :] = lat[:, lane * 128 : (lane + 1) * 128]
            return carry

        lax.fori_loop(0, ord_dev, transform, 0, unroll=2)

        def pack(row, carry):
            which, shell = row // shells, row % shells
            part, local = shell // mine, shell % mine
            for lane in range(lanes):
                picked = rows_ref[lane, pl.ds(row, modes, stride=2 * shells), :]
                send_ref[chunk, part, which, local, :, lane * 128 : (lane + 1) * 128] = (
                    picked.astype(jnp.bfloat16)
                )
            return carry

        lax.fori_loop(0, 2 * shells, pack, 0, unroll=4)
        recv_ref[chunk, me] = send_ref[chunk, me]
        if chunk == 0:
            pl.semaphore_wait(barrier, parts + rings - 2)
        for hop in range(1, parts):
            lat_copy(chunk, hop, me).start()

    for chunk in range(chunks):
        for hop in range(1, parts):
            lat_copy(chunk, hop, lax.rem(me + parts - hop, parts)).wait_recv()

        def multiply(local, carry):
            grids = []
            for which in range(2):
                lat = jnp.concatenate(
                    [recv_ref[chunk, part, which, local] for part in range(parts)], axis=0
                )
                grids.append(jnp.dot(synth_ref[...], lat, preferred_element_type=jnp.float32))
            product = (grids[0] * grids[1]).astype(jnp.bfloat16)
            back = jnp.dot(analysis_ref[...], product, preferred_element_type=jnp.float32) * scale
            for part in range(parts):
                back_send_ref[chunk, part, local] = back[part * modes : (part + 1) * modes].astype(
                    jnp.bfloat16
                )
            return carry

        lax.fori_loop(0, mine, multiply, 0)
        back_recv_ref[chunk, me] = back_send_ref[chunk, me]
        for hop in range(1, parts):
            back_copy(chunk, hop, me).start()

    for chunk in range(chunks):
        for hop in range(1, parts):
            back_copy(chunk, hop, lax.rem(me + parts - hop, parts)).wait_recv()

        def widen(shell, carry):
            base = pl.multiple_of(shell * modes, modes)
            for lane in range(lanes):
                wide_ref[lane, pl.ds(base, modes), :] = back_recv_ref[
                    chunk, shell // mine, shell % mine, :, lane * 128 : (lane + 1) * 128
                ].astype(jnp.float32)
            return carry

        lax.fori_loop(0, shells, widen, 0, unroll=4)

        def untransform(order, carry):
            picked = jnp.concatenate(
                [
                    jnp.concatenate(
                        [
                            wide_ref[lane, pl.ds(2 * order + half, shells, stride=modes), :].astype(
                                jnp.bfloat16
                            )
                            for lane in range(lanes)
                        ],
                        axis=1,
                    )
                    for half in range(2)
                ],
                axis=0,
            )
            forcing = lax.dot_general(
                picked, table_ref[chunk, order], (((1,), (1,)), ((), ())),
                preferred_element_type=jnp.float32,
            )
            if chunk > 0:
                forcing = sum_ref[order] + forcing
            if chunk < chunks - 1:
                sum_ref[order] = forcing
                return carry
            for half in range(2):
                right = field_ref[:, order, half, :] + forcing[half * shells : (half + 1) * shells]
                for block in range(blocks):
                    right_ref[block, pl.ds(half * ord_dev + order, shells, stride=modes), :] = right[
                        :, block * 128 : (block + 1) * 128
                    ]
            return carry

        lax.fori_loop(0, ord_dev, untransform, 0, unroll=2)

    offset = nr_total * 7 // 13
    cut = [slice(block * 128, (block + 1) * 128) for block in range(blocks)]
    tile = (ord_dev, 128)
    angulars = []
    for block in range(blocks):
        degree = (
            me * ord_dev
            + block * 128
            + lax.broadcasted_iota(jnp.int32, tile, 0)
            + lax.broadcasted_iota(jnp.int32, tile, 1)
        ).astype(jnp.float32)
        angulars.append(degree * (degree + 1.0))

    def forward(shell, carry):
        index = ring * shells + shell
        kappa = jnp.full(tile, kappa_ref[shell], jnp.float32)
        spot = jnp.full(tile, index, jnp.int32)
        lower = jnp.where(spot > 0, -kappa, 0.0)
        upper = jnp.where(spot < nr_total - 1, -kappa, 0.0)
        radius = (offset + spot).astype(jnp.float32)
        weight = kappa / (radius * radius)
        start = pl.multiple_of(shell * modes, modes)
        new = []
        for block in range(blocks):
            ratio, value0, value1, pull = carry[block]
            diagonal = 1.0 + 2.0 * kappa + weight * angulars[block]
            inverse = 1.0 / (diagonal - lower * ratio)
            ratio = upper * inverse
            value0 = (right_ref[block, pl.ds(start, ord_dev), :] - lower * value0) * inverse
            value1 = (
                right_ref[block, pl.ds(start + ord_dev, ord_dev), :] - lower * value1
            ) * inverse
            pull = -lower * pull * inverse
            alpha_ref[shell, :ord_dev, cut[block]] = value0
            alpha_ref[shell, ord_dev:, cut[block]] = value1
            beta_ref[shell, :, cut[block]] = pull
            gamma_ref[shell, :, cut[block]] = ratio
            new.append((ratio, value0, value1, pull))
        return tuple(new)

    blank = jnp.zeros(tile, jnp.float32)
    unity = jnp.ones(tile, jnp.float32)
    outset = tuple((blank, blank, blank, unity) for _ in range(blocks))
    lax.fori_loop(0, shells, forward, outset)

    def backward(step, carry):
        shell = shells - 1 - step
        new = []
        for block in range(blocks):
            alpha0, alpha1, beta, gamma = carry[block]
            ratio = gamma_ref[shell, :, cut[block]]
            alpha0 = alpha_ref[shell, :ord_dev, cut[block]] - ratio * alpha0
            alpha1 = alpha_ref[shell, ord_dev:, cut[block]] - ratio * alpha1
            beta = beta_ref[shell, :, cut[block]] - ratio * beta
            gamma = -ratio * gamma
            alpha_ref[shell, :ord_dev, cut[block]] = alpha0
            alpha_ref[shell, ord_dev:, cut[block]] = alpha1
            beta_ref[shell, :, cut[block]] = beta
            gamma_ref[shell, :, cut[block]] = gamma
            new.append((alpha0, alpha1, beta, gamma))
        return tuple(new)

    lax.fori_loop(0, shells, backward, outset)

    for side, shell in enumerate((0, shells - 1)):
        edge_ref[4 * side] = alpha_ref[shell, :ord_dev]
        edge_ref[4 * side + 1] = alpha_ref[shell, ord_dev:]
        edge_ref[4 * side + 2] = beta_ref[shell]
        edge_ref[4 * side + 3] = gamma_ref[shell]
    edges_ref[ring] = edge_ref[...]
    for hop in range(1, rings):
        edge_copy(hop, ring).start()
    for hop in range(1, rings):
        edge_copy(hop, lax.rem(ring + rings - hop, rings)).wait_recv()

    spot = jnp.full(tile, ring, jnp.int32)
    for block in range(blocks):
        known, slope = [blank, blank], blank
        lefts, firsts = [], []
        for device in range(rings):
            head = [edges_ref[device, k, :, cut[block]] for k in range(4)]
            tail = [edges_ref[device, 4 + k, :, cut[block]] for k in range(4)]
            lefts.append((known, slope))
            inverse = 1.0 / (1.0 - head[2] * slope)
            const = [(head[c] + head[2] * known[c]) * inverse for c in range(2)]
            gain = head[3] * inverse
            firsts.append((const, gain))
            known = [tail[c] + tail[2] * (known[c] + slope * const[c]) for c in range(2)]
            slope = tail[3] + tail[2] * slope * gain
        beyond, before, after = [blank, blank], [blank, blank], [blank, blank]
        for device in reversed(range(rings)):
            const, gain = firsts[device]
            left, tilt = lefts[device]
            here = spot == device
            start = [const[c] + gain * beyond[c] for c in range(2)]
            before = [jnp.where(here, left[c] + tilt * start[c], before[c]) for c in range(2)]
            after = [jnp.where(here, beyond[c], after[c]) for c in range(2)]
            beyond = start

        def emit(shell, carry):
            beta, gamma = beta_ref[shell, :, cut[block]], gamma_ref[shell, :, cut[block]]
            for half in range(2):
                out_ref[shell, :, half, cut[block]] = (
                    alpha_ref[shell, half * ord_dev : (half + 1) * ord_dev, cut[block]]
                    + beta * before[half]
                    + gamma * after[half]
                )
            return carry

        lax.fori_loop(0, shells, emit, 0, unroll=2)

    for chunk in range(chunks):
        for hop in range(1, parts):
            lat_copy(chunk, hop, me).wait_send()
            back_copy(chunk, hop, me).wait_send()
    for hop in range(1, rings):
        edge_copy(hop, ring).wait_send()


def on_device(scalar_field, radial_flow, legendre, diffusivity):
    shells, ord_dev, _, degrees = scalar_field.shape
    lats = legendre.shape[2]
    parts, rings = lax.axis_size("mode"), lax.axis_size("radial")
    orders = ord_dev * parts
    modes = 2 * ord_dev
    mine = shells // parts
    synth, analysis, scale = longitude_tables(orders)
    width = 256 if lats % 256 == 0 else lats
    chunks = lats // width
    lanes, blocks = width // 128, degrees // 128
    bf16, f32 = jnp.bfloat16, jnp.float32
    vmem = pl.BlockSpec(memory_space=pltpu.VMEM)
    dma = pltpu.SemaphoreType.DMA
    return pl.pallas_call(
        functools.partial(whole_step, chunks, scale),
        in_specs=[
            pl.BlockSpec(memory_space=pltpu.SMEM),
            pl.BlockSpec(memory_space=pl.ANY),
            vmem, vmem, vmem, vmem,
        ],
        out_specs=vmem,
        out_shape=jax.ShapeDtypeStruct(scalar_field.shape, f32),
        scratch_shapes=[
            pltpu.VMEM((chunks, ord_dev, degrees, width), bf16),
            pltpu.VMEM((ord_dev, 4 * shells, degrees), bf16),
            pltpu.VMEM((lanes, 4 * shells * ord_dev, 128), f32),
            pltpu.VMEM((chunks, parts, 2, mine, modes, width), bf16),
            pltpu.VMEM((chunks, parts, 2, mine, modes, width), bf16),
            pltpu.VMEM((chunks, parts, mine, modes, width), bf16),
            pltpu.VMEM((chunks, parts, mine, modes, width), bf16),
            pltpu.VMEM((lanes, shells * modes, 128), f32),
            pltpu.VMEM((ord_dev, 2 * shells, degrees), f32),
            pltpu.VMEM((blocks, shells * modes, 128), f32),
            pltpu.VMEM((shells, modes, degrees), f32),
            pltpu.VMEM((shells, ord_dev, degrees), f32),
            pltpu.VMEM((shells, ord_dev, degrees), f32),
            pltpu.VMEM((8, ord_dev, degrees), f32),
            pltpu.VMEM((rings, 8, ord_dev, degrees), f32),
            dma((chunks,)),
            dma((chunks, parts - 1)),
            dma((chunks, parts - 1)),
            dma((chunks, parts - 1)),
            dma((chunks, parts - 1)),
            dma((rings - 1,)),
            dma((rings - 1,)),
        ],
        compiler_params=params(collective_id=0, has_side_effects=True),
        name="whole_step",
    )(diffusivity, legendre, scalar_field, radial_flow, synth, analysis)


def solution(mesh):
    return jax.shard_map(
        on_device,
        mesh=mesh,
        in_specs=(
            P("radial", "mode", None, None),
            P("radial", "mode", None, None),
            P("mode", None, None),
            P("radial"),
        ),
        out_specs=P("radial", "mode", None, None),
        check_vma=False,
    )
```

```python
import functools
import math

import jax
import jax.numpy as jnp
import numpy as np
from jax import lax
from jax.experimental import pallas as pl
from jax.experimental.pallas import tpu as pltpu
from jax.sharding import PartitionSpec as P

NLON = 1536
VMEM_LIMIT = 60 * 1024 * 1024


def params(**more):
    return pltpu.CompilerParams(vmem_limit_bytes=VMEM_LIMIT, **more)


def grid_points(orders):
    needed = 3 * (orders - 1) + 1
    return next(q for q in range(128, NLON + 1, 128) if q >= needed and NLON % q == 0)


def longitude_tables(orders):
    points = grid_points(orders)
    stride = NLON // points
    phase = np.arange(orders)[:, None] * (np.arange(points) * stride)[None, :] % NLON
    angle = phase.astype(np.float32) * np.float32(2.0 * math.pi / NLON)
    paired = np.stack([np.cos(angle), -np.sin(angle)], axis=1).reshape(2 * orders, points)
    synth = (paired / np.float32(math.sqrt(orders))).astype(jnp.bfloat16)
    analysis = (paired * np.float32(math.sqrt(2.0 / NLON))).astype(jnp.bfloat16)
    return jnp.asarray(synth.T), jnp.asarray(analysis), float(stride)


def whole_step(
    chunks, scale, kappa_ref, table_hbm, field_ref, flow_ref, synth_ref, analysis_ref, out_ref,
    table_ref, spectral_ref, rows_ref, send_ref, recv_ref, back_send_ref, back_recv_ref,
    wide_ref, sum_ref, right_ref, alpha_ref, beta_ref, gamma_ref,
    ratio_ref, inverse_ref, slope_ref, slopes_ref, edge_ref, edges_ref,
    table_sem, send_sem, recv_sem, back_send_sem, back_recv_sem, slope_send_sem, slope_recv_sem,
    edge_send_sem, edge_recv_sem,
):
    shells, ord_dev, _, degrees = field_ref.shape
    modes = 2 * ord_dev
    parts, rings = lax.axis_size("mode"), lax.axis_size("radial")
    me, ring = lax.axis_index("mode"), lax.axis_index("radial")
    mine = shells // parts
    count = 4 * shells
    width = table_ref.shape[3]
    lanes, blocks = width // 128, degrees // 128
    nr_total = shells * rings
    group = 2 if width < 256 and mine % 2 == 0 else 1

    def table_copy(chunk):
        return pltpu.make_async_copy(
            table_hbm.at[:, :, pl.ds(chunk * width, width)], table_ref.at[chunk], table_sem.at[chunk]
        )

    for chunk in range(chunks):
        table_copy(chunk).start()

    barrier = pltpu.get_barrier_semaphore()
    for hop in range(1, parts):
        pl.semaphore_signal(
            barrier, inc=1, device_id={"mode": lax.rem(me + hop, parts)},
            device_id_type=pl.DeviceIdType.MESH,
        )
    for hop in range(1, rings):
        pl.semaphore_signal(
            barrier, inc=1, device_id={"radial": lax.rem(ring + hop, rings)},
            device_id_type=pl.DeviceIdType.MESH,
        )

    def exchange(axis, hop, source, target, send, receive):
        here, size = (me, parts) if axis == "mode" else (ring, rings)
        return pltpu.make_async_remote_copy(
            src_ref=source, dst_ref=target, send_sem=send, recv_sem=receive,
            device_id={axis: lax.rem(here + hop, size)}, device_id_type=pl.DeviceIdType.MESH,
        )

    def lat_copy(chunk, hop, slot):
        to = lax.rem(me + hop, parts)
        return exchange(
            "mode", hop, send_ref.at[chunk, to], recv_ref.at[chunk, slot],
            send_sem.at[chunk, hop - 1], recv_sem.at[chunk, hop - 1],
        )

    def back_copy(chunk, hop, slot):
        to = lax.rem(me + hop, parts)
        return exchange(
            "mode", hop, back_send_ref.at[chunk, to], back_recv_ref.at[chunk, slot],
            back_send_sem.at[chunk, hop - 1], back_recv_sem.at[chunk, hop - 1],
        )

    def edge_copy(hop, slot):
        return exchange(
            "radial", hop, edge_ref, edges_ref.at[slot],
            edge_send_sem.at[hop - 1], edge_recv_sem.at[hop - 1],
        )

    def slope_copy(hop, slot):
        return exchange(
            "radial", hop, slope_ref, slopes_ref.at[slot],
            slope_send_sem.at[hop - 1], slope_recv_sem.at[hop - 1],
        )

    def stack(order, carry):
        spectral_ref[order] = jnp.concatenate(
            [ref[:, order, half, :] for half in range(2) for ref in (field_ref, flow_ref)], axis=0
        ).astype(jnp.bfloat16)
        return carry

    lax.fori_loop(0, ord_dev, stack, 0, unroll=2)

    for chunk in range(chunks):
        table_copy(chunk).wait()

        def transform(order, carry):
            lat = jnp.dot(
                spectral_ref[order], table_ref[chunk, order], preferred_element_type=jnp.float32
            )
            base = pl.multiple_of(order * count, count)
            for lane in range(lanes):
                rows_ref[lane, pl.ds(base, count), :] = lat[:, lane * 128 : (lane + 1) * 128]
            return carry

        lax.fori_loop(0, ord_dev, transform, 0, unroll=2)

        def pack(row, carry):
            which, shell = row // shells, row % shells
            part, local = shell // mine, shell % mine
            for lane in range(lanes):
                picked = rows_ref[lane, pl.ds(row, modes, stride=2 * shells), :]
                send_ref[chunk, part, which, local, :, lane * 128 : (lane + 1) * 128] = (
                    picked.astype(jnp.bfloat16)
                )
            return carry

        lax.fori_loop(0, 2 * shells, pack, 0, unroll=4)
        recv_ref[chunk, me] = send_ref[chunk, me]
        if chunk == 0:
            pl.semaphore_wait(barrier, parts + rings - 2)
        for hop in range(1, parts):
            lat_copy(chunk, hop, me).start()

    offset = nr_total * 7 // 13
    cut = [slice(block * 128, (block + 1) * 128) for block in range(blocks)]
    tile = (ord_dev, 128)
    blank = jnp.zeros(tile, jnp.float32)
    unity = jnp.ones(tile, jnp.float32)
    angulars = []
    for block in range(blocks):
        degree = (
            me * ord_dev
            + block * 128
            + lax.broadcasted_iota(jnp.int32, tile, 0)
            + lax.broadcasted_iota(jnp.int32, tile, 1)
        ).astype(jnp.float32)
        angulars.append(degree * (degree + 1.0))

    def factor(shell, carry):
        kappa = jnp.full(tile, kappa_ref[shell], jnp.float32)
        spot = jnp.full(tile, ring * shells + shell, jnp.int32)
        lower = jnp.where(spot > 0, -kappa, 0.0)
        upper = jnp.where(spot < nr_total - 1, -kappa, 0.0)
        radius = (offset + spot).astype(jnp.float32)
        weight = kappa / (radius * radius)
        new = []
        for block in range(blocks):
            ratio, pull = carry[block]
            diagonal = 1.0 + 2.0 * kappa + weight * angulars[block]
            inverse = 1.0 / (diagonal - lower * ratio)
            ratio = upper * inverse
            pull = -lower * pull * inverse
            inverse_ref[shell, :, cut[block]] = inverse
            ratio_ref[shell, :, cut[block]] = ratio
            beta_ref[shell, :, cut[block]] = pull
            new.append((ratio, pull))
        return tuple(new)

    outset = tuple((blank, unity) for _ in range(blocks))
    lax.fori_loop(0, shells, factor, outset)

    def unfactor(step, carry):
        shell = shells - 1 - step
        new = []
        for block in range(blocks):
            beta, gamma = carry[block]
            ratio = ratio_ref[shell, :, cut[block]]
            beta = beta_ref[shell, :, cut[block]] - ratio * beta
            gamma = -ratio * gamma
            beta_ref[shell, :, cut[block]] = beta
            gamma_ref[shell, :, cut[block]] = gamma
            new.append((beta, gamma))
        return tuple(new)

    lax.fori_loop(0, shells, unfactor, outset)
    for side, shell in enumerate((0, shells - 1)):
        slope_ref[2 * side] = beta_ref[shell]
        slope_ref[2 * side + 1] = gamma_ref[shell]
    slopes_ref[ring] = slope_ref[...]
    for hop in range(1, rings):
        slope_copy(hop, ring).start()

    for chunk in range(chunks):
        for hop in range(1, parts):
            lat_copy(chunk, hop, lax.rem(me + parts - hop, parts)).wait_recv()

        def multiply(step, carry):
            locals_ = [step * group + k for k in range(group)]
            grids = []
            for which in range(2):
                lat = jnp.concatenate(
                    [
                        jnp.concatenate(
                            [recv_ref[chunk, part, which, local] for part in range(parts)], axis=0
                        )
                        for local in locals_
                    ],
                    axis=1,
                )
                grids.append(jnp.dot(synth_ref[...], lat, preferred_element_type=jnp.float32))
            product = (grids[0] * grids[1]).astype(jnp.bfloat16)
            back = jnp.dot(analysis_ref[...], product, preferred_element_type=jnp.float32) * scale
            for k, local in enumerate(locals_):
                for part in range(parts):
                    back_send_ref[chunk, part, local] = back[
                        part * modes : (part + 1) * modes, k * width : (k + 1) * width
                    ].astype(jnp.bfloat16)
            return carry

        lax.fori_loop(0, mine // group, multiply, 0)
        back_recv_ref[chunk, me] = back_send_ref[chunk, me]
        for hop in range(1, parts):
            back_copy(chunk, hop, me).start()

    for chunk in range(chunks):
        for hop in range(1, parts):
            back_copy(chunk, hop, lax.rem(me + parts - hop, parts)).wait_recv()

        def widen(shell, carry):
            base = pl.multiple_of(shell * modes, modes)
            for lane in range(lanes):
                wide_ref[lane, pl.ds(base, modes), :] = back_recv_ref[
                    chunk, shell // mine, shell % mine, :, lane * 128 : (lane + 1) * 128
                ].astype(jnp.float32)
            return carry

        lax.fori_loop(0, shells, widen, 0, unroll=4)

        def untransform(order, carry):
            picked = jnp.concatenate(
                [
                    jnp.concatenate(
                        [
                            wide_ref[lane, pl.ds(2 * order + half, shells, stride=modes), :].astype(
                                jnp.bfloat16
                            )
                            for lane in range(lanes)
                        ],
                        axis=1,
                    )
                    for half in range(2)
                ],
                axis=0,
            )
            forcing = lax.dot_general(
                picked, table_ref[chunk, order], (((1,), (1,)), ((), ())),
                preferred_element_type=jnp.float32,
            )
            if chunk > 0:
                forcing = sum_ref[order] + forcing
            if chunk < chunks - 1:
                sum_ref[order] = forcing
                return carry
            for half in range(2):
                right = field_ref[:, order, half, :] + forcing[half * shells : (half + 1) * shells]
                for block in range(blocks):
                    right_ref[block, pl.ds(half * ord_dev + order, shells, stride=modes), :] = right[
                        :, block * 128 : (block + 1) * 128
                    ]
            return carry

        lax.fori_loop(0, ord_dev, untransform, 0, unroll=2)

    def forward(shell, carry):
        index = ring * shells + shell
        lower = jnp.where(jnp.full(tile, index, jnp.int32) > 0, -kappa_ref[shell], 0.0)
        start = pl.multiple_of(shell * modes, modes)
        new = []
        for block in range(blocks):
            inverse = inverse_ref[shell, :, cut[block]]
            value0 = (
                right_ref[block, pl.ds(start, ord_dev), :] - lower * carry[block][0]
            ) * inverse
            value1 = (
                right_ref[block, pl.ds(start + ord_dev, ord_dev), :] - lower * carry[block][1]
            ) * inverse
            alpha_ref[shell, :ord_dev, cut[block]] = value0
            alpha_ref[shell, ord_dev:, cut[block]] = value1
            new.append((value0, value1))
        return tuple(new)

    empty = tuple((blank, blank) for _ in range(blocks))
    lax.fori_loop(0, shells, forward, empty, unroll=4)

    def backward(step, carry):
        shell = shells - 1 - step
        new = []
        for block in range(blocks):
            ratio = ratio_ref[shell, :, cut[block]]
            alpha0 = alpha_ref[shell, :ord_dev, cut[block]] - ratio * carry[block][0]
            alpha1 = alpha_ref[shell, ord_dev:, cut[block]] - ratio * carry[block][1]
            alpha_ref[shell, :ord_dev, cut[block]] = alpha0
            alpha_ref[shell, ord_dev:, cut[block]] = alpha1
            new.append((alpha0, alpha1))
        return tuple(new)

    lax.fori_loop(0, shells, backward, empty, unroll=4)

    for side, shell in enumerate((0, shells - 1)):
        edge_ref[2 * side] = alpha_ref[shell, :ord_dev]
        edge_ref[2 * side + 1] = alpha_ref[shell, ord_dev:]
    edges_ref[ring] = edge_ref[...]
    for hop in range(1, rings):
        edge_copy(hop, ring).start()
    for hop in range(1, rings):
        slope_copy(hop, lax.rem(ring + rings - hop, rings)).wait_recv()
    for hop in range(1, rings):
        edge_copy(hop, lax.rem(ring + rings - hop, rings)).wait_recv()

    spot = jnp.full(tile, ring, jnp.int32)
    for block in range(blocks):
        known, slope = [blank, blank], blank
        lefts, firsts = [], []
        for device in range(rings):
            head = [ref[device, k, :, cut[block]] for ref in (edges_ref, slopes_ref) for k in (0, 1)]
            tail = [ref[device, k, :, cut[block]] for ref in (edges_ref, slopes_ref) for k in (2, 3)]
            lefts.append((known, slope))
            inverse = 1.0 / (1.0 - head[2] * slope)
            const = [(head[c] + head[2] * known[c]) * inverse for c in range(2)]
            gain = head[3] * inverse
            firsts.append((const, gain))
            known = [tail[c] + tail[2] * (known[c] + slope * const[c]) for c in range(2)]
            slope = tail[3] + tail[2] * slope * gain
        beyond, before, after = [blank, blank], [blank, blank], [blank, blank]
        for device in reversed(range(rings)):
            const, gain = firsts[device]
            left, tilt = lefts[device]
            here = spot == device
            start = [const[c] + gain * beyond[c] for c in range(2)]
            before = [jnp.where(here, left[c] + tilt * start[c], before[c]) for c in range(2)]
            after = [jnp.where(here, beyond[c], after[c]) for c in range(2)]
            beyond = start

        def emit(shell, carry):
            beta, gamma = beta_ref[shell, :, cut[block]], gamma_ref[shell, :, cut[block]]
            for half in range(2):
                out_ref[shell, :, half, cut[block]] = (
                    alpha_ref[shell, half * ord_dev : (half + 1) * ord_dev, cut[block]]
                    + beta * before[half]
                    + gamma * after[half]
                )
            return carry

        lax.fori_loop(0, shells, emit, 0, unroll=2)

    for chunk in range(chunks):
        for hop in range(1, parts):
            lat_copy(chunk, hop, me).wait_send()
            back_copy(chunk, hop, me).wait_send()
    for hop in range(1, rings):
        slope_copy(hop, ring).wait_send()
        edge_copy(hop, ring).wait_send()


def on_device(scalar_field, radial_flow, legendre, diffusivity):
    shells, ord_dev, _, degrees = scalar_field.shape
    lats = legendre.shape[2]
    parts, rings = lax.axis_size("mode"), lax.axis_size("radial")
    orders = ord_dev * parts
    modes = 2 * ord_dev
    mine = shells // parts
    synth, analysis, scale = longitude_tables(orders)
    width = 128 if lats % 128 == 0 else lats
    chunks = lats // width
    lanes, blocks = width // 128, degrees // 128
    bf16, f32 = jnp.bfloat16, jnp.float32
    vmem = pl.BlockSpec(memory_space=pltpu.VMEM)
    dma = pltpu.SemaphoreType.DMA
    return pl.pallas_call(
        functools.partial(whole_step, chunks, scale),
        in_specs=[
            pl.BlockSpec(memory_space=pltpu.SMEM),
            pl.BlockSpec(memory_space=pl.ANY),
            vmem, vmem, vmem, vmem,
        ],
        out_specs=vmem,
        out_shape=jax.ShapeDtypeStruct(scalar_field.shape, f32),
        scratch_shapes=[
            pltpu.VMEM((chunks, ord_dev, degrees, width), bf16),
            pltpu.VMEM((ord_dev, 4 * shells, degrees), bf16),
            pltpu.VMEM((lanes, 4 * shells * ord_dev, 128), f32),
            pltpu.VMEM((chunks, parts, 2, mine, modes, width), bf16),
            pltpu.VMEM((chunks, parts, 2, mine, modes, width), bf16),
            pltpu.VMEM((chunks, parts, mine, modes, width), bf16),
            pltpu.VMEM((chunks, parts, mine, modes, width), bf16),
            pltpu.VMEM((lanes, shells * modes, 128), f32),
            pltpu.VMEM((ord_dev, 2 * shells, degrees), f32),
            pltpu.VMEM((blocks, shells * modes, 128), f32),
            pltpu.VMEM((shells, modes, degrees), f32),
            pltpu.VMEM((shells, ord_dev, degrees), f32),
            pltpu.VMEM((shells, ord_dev, degrees), f32),
            pltpu.VMEM((shells, ord_dev, degrees), f32),
            pltpu.VMEM((shells, ord_dev, degrees), f32),
            pltpu.VMEM((4, ord_dev, degrees), f32),
            pltpu.VMEM((rings, 4, ord_dev, degrees), f32),
            pltpu.VMEM((4, ord_dev, degrees), f32),
            pltpu.VMEM((rings, 4, ord_dev, degrees), f32),
            dma((chunks,)),
            dma((chunks, parts - 1)),
            dma((chunks, parts - 1)),
            dma((chunks, parts - 1)),
            dma((chunks, parts - 1)),
            dma((rings - 1,)),
            dma((rings - 1,)),
            dma((rings - 1,)),
            dma((rings - 1,)),
        ],
        compiler_params=params(collective_id=0, has_side_effects=True),
        name="whole_step",
    )(diffusivity, legendre, scalar_field, radial_flow, synth, analysis)


def solution(mesh):
    return jax.shard_map(
        on_device,
        mesh=mesh,
        in_specs=(
            P("radial", "mode", None, None),
            P("radial", "mode", None, None),
            P("mode", None, None),
            P("radial"),
        ),
        out_specs=P("radial", "mode", None, None),
        check_vma=False,
    )
```

```python
import functools
import math

import jax
import jax.numpy as jnp
import numpy as np
from jax import lax
from jax.experimental import pallas as pl
from jax.experimental.pallas import tpu as pltpu
from jax.sharding import PartitionSpec as P

NLON = 1536
VMEM_LIMIT = 60 * 1024 * 1024


def params(**more):
    return pltpu.CompilerParams(vmem_limit_bytes=VMEM_LIMIT, **more)


def grid_points(orders):
    needed = 3 * (orders - 1) + 1
    return next(q for q in range(128, NLON + 1, 128) if q >= needed and NLON % q == 0)


def longitude_tables(orders):
    points = grid_points(orders)
    stride = NLON // points
    phase = np.arange(orders)[:, None] * (np.arange(points) * stride)[None, :] % NLON
    angle = phase.astype(np.float32) * np.float32(2.0 * math.pi / NLON)
    paired = np.stack([np.cos(angle), -np.sin(angle)], axis=1).reshape(2 * orders, points)
    synth = (paired / np.float32(math.sqrt(orders))).astype(jnp.bfloat16)
    analysis = (paired * np.float32(math.sqrt(2.0 / NLON))).astype(jnp.bfloat16)
    return jnp.asarray(synth.T), jnp.asarray(analysis), float(stride)


def partner(here, hop, size):
    place, bit = 0, 1
    while bit < size:
        place = place + (here // bit + hop // bit) % 2 * bit
        bit *= 2
    return place


def whole_step(
    chunks, scale, kappa_ref, table_hbm, field_ref, flow_ref, synth_ref, analysis_ref, out_ref,
    table_ref, spectral_ref, rows_ref, send_ref, recv_ref, back_send_ref, back_recv_ref,
    wide_ref, sum_ref, right_ref, alpha_ref, beta_ref, gamma_ref,
    ratio_ref, inverse_ref, slope_ref, slopes_ref, edge_ref, edges_ref,
    table_sem, send_sem, recv_sem, back_send_sem, back_recv_sem, slope_send_sem, slope_recv_sem,
    edge_send_sem, edge_recv_sem,
):
    shells, ord_dev, _, degrees = field_ref.shape
    modes = 2 * ord_dev
    parts, rings = lax.axis_size("mode"), lax.axis_size("radial")
    me, ring = lax.axis_index("mode"), lax.axis_index("radial")
    mine = shells // parts
    count = 4 * shells
    width = table_ref.shape[3]
    lanes, blocks = width // 128, degrees // 128
    nr_total = shells * rings
    group = 2 if width < 256 and mine % 2 == 0 else 1

    def table_copy(chunk):
        return pltpu.make_async_copy(
            table_hbm.at[:, :, pl.ds(chunk * width, width)], table_ref.at[chunk], table_sem.at[chunk]
        )

    for chunk in range(chunks):
        table_copy(chunk).start()

    barrier = pltpu.get_barrier_semaphore()
    for hop in range(1, parts):
        pl.semaphore_signal(
            barrier, inc=1, device_id={"mode": partner(me, hop, parts)},
            device_id_type=pl.DeviceIdType.MESH,
        )
    for hop in range(1, rings):
        pl.semaphore_signal(
            barrier, inc=1, device_id={"radial": partner(ring, hop, rings)},
            device_id_type=pl.DeviceIdType.MESH,
        )

    def exchange(axis, to, source, target, send, receive):
        return pltpu.make_async_remote_copy(
            src_ref=source, dst_ref=target, send_sem=send, recv_sem=receive,
            device_id={axis: to}, device_id_type=pl.DeviceIdType.MESH,
        )

    def lat_copy(chunk, hop, slot):
        to = partner(me, hop, parts)
        return exchange(
            "mode", to, send_ref.at[chunk, to], recv_ref.at[chunk, slot],
            send_sem.at[chunk, hop - 1], recv_sem.at[chunk, hop - 1],
        )

    def back_copy(chunk, hop, slot):
        to = partner(me, hop, parts)
        return exchange(
            "mode", to, back_send_ref.at[chunk, to], back_recv_ref.at[chunk, slot],
            back_send_sem.at[chunk, hop - 1], back_recv_sem.at[chunk, hop - 1],
        )

    def edge_copy(hop, slot):
        return exchange(
            "radial", partner(ring, hop, rings), edge_ref, edges_ref.at[slot],
            edge_send_sem.at[hop - 1], edge_recv_sem.at[hop - 1],
        )

    def slope_copy(hop, slot):
        return exchange(
            "radial", partner(ring, hop, rings), slope_ref, slopes_ref.at[slot],
            slope_send_sem.at[hop - 1], slope_recv_sem.at[hop - 1],
        )

    def stack(order, carry):
        spectral_ref[order] = jnp.concatenate(
            [ref[:, order, half, :] for half in range(2) for ref in (field_ref, flow_ref)], axis=0
        ).astype(jnp.bfloat16)
        return carry

    lax.fori_loop(0, ord_dev, stack, 0, unroll=2)

    for chunk in range(chunks):
        table_copy(chunk).wait()

        def transform(order, carry):
            lat = jnp.dot(
                spectral_ref[order], table_ref[chunk, order], preferred_element_type=jnp.float32
            )
            base = pl.multiple_of(order * count, count)
            for lane in range(lanes):
                rows_ref[lane, pl.ds(base, count), :] = lat[:, lane * 128 : (lane + 1) * 128]
            return carry

        lax.fori_loop(0, ord_dev, transform, 0, unroll=2)

        def pack(row, carry):
            which, shell = row // shells, row % shells
            part, local = shell // mine, shell % mine
            for lane in range(lanes):
                picked = rows_ref[lane, pl.ds(row, modes, stride=2 * shells), :]
                send_ref[chunk, part, which, local, :, lane * 128 : (lane + 1) * 128] = (
                    picked.astype(jnp.bfloat16)
                )
            return carry

        lax.fori_loop(0, 2 * shells, pack, 0, unroll=4)
        recv_ref[chunk, me] = send_ref[chunk, me]
        if chunk == 0:
            pl.semaphore_wait(barrier, parts + rings - 2)
        near = parts if chunk < 2 else parts // 2
        for hop in range(1, near):
            lat_copy(chunk, hop, me).start()

    for chunk in range(2, chunks):
        for hop in range(parts // 2, parts):
            lat_copy(chunk, hop, me).start()

    offset = nr_total * 7 // 13
    cut = [slice(block * 128, (block + 1) * 128) for block in range(blocks)]
    tile = (ord_dev, 128)
    blank = jnp.zeros(tile, jnp.float32)
    unity = jnp.ones(tile, jnp.float32)
    angulars = []
    for block in range(blocks):
        degree = (
            me * ord_dev
            + block * 128
            + lax.broadcasted_iota(jnp.int32, tile, 0)
            + lax.broadcasted_iota(jnp.int32, tile, 1)
        ).astype(jnp.float32)
        angulars.append(degree * (degree + 1.0))

    def factor(shell, carry):
        kappa = jnp.full(tile, kappa_ref[shell], jnp.float32)
        spot = jnp.full(tile, ring * shells + shell, jnp.int32)
        lower = jnp.where(spot > 0, -kappa, 0.0)
        upper = jnp.where(spot < nr_total - 1, -kappa, 0.0)
        radius = (offset + spot).astype(jnp.float32)
        weight = kappa / (radius * radius)
        new = []
        for block in range(blocks):
            ratio, pull = carry[block]
            diagonal = 1.0 + 2.0 * kappa + weight * angulars[block]
            inverse = 1.0 / (diagonal - lower * ratio)
            ratio = upper * inverse
            pull = -lower * pull * inverse
            inverse_ref[shell, :, cut[block]] = inverse
            ratio_ref[shell, :, cut[block]] = ratio
            beta_ref[shell, :, cut[block]] = pull
            new.append((ratio, pull))
        return tuple(new)

    outset = tuple((blank, unity) for _ in range(blocks))
    lax.fori_loop(0, shells, factor, outset)

    def unfactor(step, carry):
        shell = shells - 1 - step
        new = []
        for block in range(blocks):
            beta, gamma = carry[block]
            ratio = ratio_ref[shell, :, cut[block]]
            beta = beta_ref[shell, :, cut[block]] - ratio * beta
            gamma = -ratio * gamma
            beta_ref[shell, :, cut[block]] = beta
            gamma_ref[shell, :, cut[block]] = gamma
            new.append((beta, gamma))
        return tuple(new)

    lax.fori_loop(0, shells, unfactor, outset)
    for side, shell in enumerate((0, shells - 1)):
        slope_ref[2 * side] = beta_ref[shell]
        slope_ref[2 * side + 1] = gamma_ref[shell]
    slopes_ref[ring] = slope_ref[...]
    for hop in range(1, rings):
        slope_copy(hop, ring).start()

    for chunk in range(chunks):
        for hop in range(1, parts):
            lat_copy(chunk, hop, partner(me, hop, parts)).wait_recv()

        def multiply(step, carry):
            locals_ = [step * group + k for k in range(group)]
            grids = []
            for which in range(2):
                lat = jnp.concatenate(
                    [
                        jnp.concatenate(
                            [recv_ref[chunk, part, which, local] for part in range(parts)], axis=0
                        )
                        for local in locals_
                    ],
                    axis=1,
                )
                grids.append(jnp.dot(synth_ref[...], lat, preferred_element_type=jnp.float32))
            product = (grids[0] * grids[1]).astype(jnp.bfloat16)
            back = jnp.dot(analysis_ref[...], product, preferred_element_type=jnp.float32) * scale
            for k, local in enumerate(locals_):
                for part in range(parts):
                    back_send_ref[chunk, part, local] = back[
                        part * modes : (part + 1) * modes, k * width : (k + 1) * width
                    ].astype(jnp.bfloat16)
            return carry

        lax.fori_loop(0, mine // group, multiply, 0)
        back_recv_ref[chunk, me] = back_send_ref[chunk, me]
        for hop in range(1, parts):
            back_copy(chunk, hop, me).start()

    for chunk in range(chunks):
        for hop in range(1, parts):
            back_copy(chunk, hop, partner(me, hop, parts)).wait_recv()

        def widen(shell, carry):
            base = pl.multiple_of(shell * modes, modes)
            for lane in range(lanes):
                wide_ref[lane, pl.ds(base, modes), :] = back_recv_ref[
                    chunk, shell // mine, shell % mine, :, lane * 128 : (lane + 1) * 128
                ].astype(jnp.float32)
            return carry

        lax.fori_loop(0, shells, widen, 0, unroll=4)

        def untransform(order, carry):
            picked = jnp.concatenate(
                [
                    jnp.concatenate(
                        [
                            wide_ref[lane, pl.ds(2 * order + half, shells, stride=modes), :].astype(
                                jnp.bfloat16
                            )
                            for lane in range(lanes)
                        ],
                        axis=1,
                    )
                    for half in range(2)
                ],
                axis=0,
            )
            forcing = lax.dot_general(
                picked, table_ref[chunk, order], (((1,), (1,)), ((), ())),
                preferred_element_type=jnp.float32,
            )
            if chunk > 0:
                forcing = sum_ref[order] + forcing
            if chunk < chunks - 1:
                sum_ref[order] = forcing
                return carry
            for half in range(2):
                right = field_ref[:, order, half, :] + forcing[half * shells : (half + 1) * shells]
                for block in range(blocks):
                    right_ref[block, pl.ds(half * ord_dev + order, shells, stride=modes), :] = right[
                        :, block * 128 : (block + 1) * 128
                    ]
            return carry

        lax.fori_loop(0, ord_dev, untransform, 0, unroll=2)

    def forward(shell, carry):
        index = ring * shells + shell
        lower = jnp.where(jnp.full(tile, index, jnp.int32) > 0, -kappa_ref[shell], 0.0)
        start = pl.multiple_of(shell * modes, modes)
        new = []
        for block in range(blocks):
            inverse = inverse_ref[shell, :, cut[block]]
            value0 = (
                right_ref[block, pl.ds(start, ord_dev), :] - lower * carry[block][0]
            ) * inverse
            value1 = (
                right_ref[block, pl.ds(start + ord_dev, ord_dev), :] - lower * carry[block][1]
            ) * inverse
            alpha_ref[shell, :ord_dev, cut[block]] = value0
            alpha_ref[shell, ord_dev:, cut[block]] = value1
            new.append((value0, value1))
        return tuple(new)

    empty = tuple((blank, blank) for _ in range(blocks))
    lax.fori_loop(0, shells, forward, empty, unroll=4)

    def backward(step, carry):
        shell = shells - 1 - step
        new = []
        for block in range(blocks):
            ratio = ratio_ref[shell, :, cut[block]]
            alpha0 = alpha_ref[shell, :ord_dev, cut[block]] - ratio * carry[block][0]
            alpha1 = alpha_ref[shell, ord_dev:, cut[block]] - ratio * carry[block][1]
            alpha_ref[shell, :ord_dev, cut[block]] = alpha0
            alpha_ref[shell, ord_dev:, cut[block]] = alpha1
            new.append((alpha0, alpha1))
        return tuple(new)

    lax.fori_loop(0, shells, backward, empty, unroll=4)

    for side, shell in enumerate((0, shells - 1)):
        edge_ref[2 * side] = alpha_ref[shell, :ord_dev]
        edge_ref[2 * side + 1] = alpha_ref[shell, ord_dev:]
    edges_ref[ring] = edge_ref[...]
    for hop in range(1, rings):
        edge_copy(hop, ring).start()
    for hop in range(1, rings):
        slope_copy(hop, partner(ring, hop, rings)).wait_recv()
    for hop in range(1, rings):
        edge_copy(hop, partner(ring, hop, rings)).wait_recv()

    spot = jnp.full(tile, ring, jnp.int32)
    for block in range(blocks):
        known, slope = [blank, blank], blank
        lefts, firsts = [], []
        for device in range(rings):
            head = [ref[device, k, :, cut[block]] for ref in (edges_ref, slopes_ref) for k in (0, 1)]
            tail = [ref[device, k, :, cut[block]] for ref in (edges_ref, slopes_ref) for k in (2, 3)]
            lefts.append((known, slope))
            inverse = 1.0 / (1.0 - head[2] * slope)
            const = [(head[c] + head[2] * known[c]) * inverse for c in range(2)]
            gain = head[3] * inverse
            firsts.append((const, gain))
            known = [tail[c] + tail[2] * (known[c] + slope * const[c]) for c in range(2)]
            slope = tail[3] + tail[2] * slope * gain
        beyond, before, after = [blank, blank], [blank, blank], [blank, blank]
        for device in reversed(range(rings)):
            const, gain = firsts[device]
            left, tilt = lefts[device]
            here = spot == device
            start = [const[c] + gain * beyond[c] for c in range(2)]
            before = [jnp.where(here, left[c] + tilt * start[c], before[c]) for c in range(2)]
            after = [jnp.where(here, beyond[c], after[c]) for c in range(2)]
            beyond = start

        def emit(shell, carry):
            beta, gamma = beta_ref[shell, :, cut[block]], gamma_ref[shell, :, cut[block]]
            for half in range(2):
                out_ref[shell, :, half, cut[block]] = (
                    alpha_ref[shell, half * ord_dev : (half + 1) * ord_dev, cut[block]]
                    + beta * before[half]
                    + gamma * after[half]
                )
            return carry

        lax.fori_loop(0, shells, emit, 0, unroll=2)

    for chunk in range(chunks):
        for hop in range(1, parts):
            lat_copy(chunk, hop, me).wait_send()
            back_copy(chunk, hop, me).wait_send()
    for hop in range(1, rings):
        slope_copy(hop, ring).wait_send()
        edge_copy(hop, ring).wait_send()


def on_device(scalar_field, radial_flow, legendre, diffusivity):
    shells, ord_dev, _, degrees = scalar_field.shape
    lats = legendre.shape[2]
    parts, rings = lax.axis_size("mode"), lax.axis_size("radial")
    orders = ord_dev * parts
    modes = 2 * ord_dev
    mine = shells // parts
    assert parts & (parts - 1) == 0 and rings & (rings - 1) == 0
    synth, analysis, scale = longitude_tables(orders)
    width = 128 if lats % 128 == 0 else lats
    chunks = lats // width
    lanes, blocks = width // 128, degrees // 128
    bf16, f32 = jnp.bfloat16, jnp.float32
    vmem = pl.BlockSpec(memory_space=pltpu.VMEM)
    dma = pltpu.SemaphoreType.DMA
    return pl.pallas_call(
        functools.partial(whole_step, chunks, scale),
        in_specs=[
            pl.BlockSpec(memory_space=pltpu.SMEM),
            pl.BlockSpec(memory_space=pl.ANY),
            vmem, vmem, vmem, vmem,
        ],
        out_specs=vmem,
        out_shape=jax.ShapeDtypeStruct(scalar_field.shape, f32),
        scratch_shapes=[
            pltpu.VMEM((chunks, ord_dev, degrees, width), bf16),
            pltpu.VMEM((ord_dev, 4 * shells, degrees), bf16),
            pltpu.VMEM((lanes, 4 * shells * ord_dev, 128), f32),
            pltpu.VMEM((chunks, parts, 2, mine, modes, width), bf16),
            pltpu.VMEM((chunks, parts, 2, mine, modes, width), bf16),
            pltpu.VMEM((chunks, parts, mine, modes, width), bf16),
            pltpu.VMEM((chunks, parts, mine, modes, width), bf16),
            pltpu.VMEM((lanes, shells * modes, 128), f32),
            pltpu.VMEM((ord_dev, 2 * shells, degrees), f32),
            pltpu.VMEM((blocks, shells * modes, 128), f32),
            pltpu.VMEM((shells, modes, degrees), f32),
            pltpu.VMEM((shells, ord_dev, degrees), f32),
            pltpu.VMEM((shells, ord_dev, degrees), f32),
            pltpu.VMEM((shells, ord_dev, degrees), f32),
            pltpu.VMEM((shells, ord_dev, degrees), f32),
            pltpu.VMEM((4, ord_dev, degrees), f32),
            pltpu.VMEM((rings, 4, ord_dev, degrees), f32),
            pltpu.VMEM((4, ord_dev, degrees), f32),
            pltpu.VMEM((rings, 4, ord_dev, degrees), f32),
            dma((chunks,)),
            dma((chunks, parts - 1)),
            dma((chunks, parts - 1)),
            dma((chunks, parts - 1)),
            dma((chunks, parts - 1)),
            dma((rings - 1,)),
            dma((rings - 1,)),
            dma((rings - 1,)),
            dma((rings - 1,)),
        ],
        compiler_params=params(collective_id=0, has_side_effects=True),
        name="whole_step",
    )(diffusivity, legendre, scalar_field, radial_flow, synth, analysis)


def solution(mesh):
    return jax.shard_map(
        on_device,
        mesh=mesh,
        in_specs=(
            P("radial", "mode", None, None),
            P("radial", "mode", None, None),
            P("mode", None, None),
            P("radial"),
        ),
        out_specs=P("radial", "mode", None, None),
        check_vma=False,
    )
```

```python
import functools
import math

import jax
import jax.numpy as jnp
import numpy as np
from jax import lax
from jax.experimental import pallas as pl
from jax.experimental.pallas import tpu as pltpu
from jax.sharding import PartitionSpec as P

NLON = 1536
VMEM_LIMIT = 60 * 1024 * 1024


def params(**more):
    return pltpu.CompilerParams(vmem_limit_bytes=VMEM_LIMIT, **more)


def grid_points(orders):
    needed = 3 * (orders - 1) + 1
    return next(q for q in range(128, NLON + 1, 128) if q >= needed and NLON % q == 0)


def longitude_tables(orders):
    points = grid_points(orders)
    stride = NLON // points
    phase = np.arange(orders)[:, None] * (np.arange(points) * stride)[None, :] % NLON
    angle = phase.astype(np.float32) * np.float32(2.0 * math.pi / NLON)
    paired = np.stack([np.cos(angle), -np.sin(angle)], axis=1).reshape(2 * orders, points)
    synth = (paired / np.float32(math.sqrt(orders))).astype(jnp.bfloat16)
    analysis = (paired * np.float32(math.sqrt(2.0 / NLON))).astype(jnp.bfloat16)
    return jnp.asarray(synth.T), jnp.asarray(analysis), float(stride)


def partner(here, hop, size):
    place, bit = 0, 1
    while bit < size:
        place = place + (here // bit + hop // bit) % 2 * bit
        bit *= 2
    return place


def whole_step(
    chunks, scale, kappa_ref, table_hbm, field_ref, flow_ref, synth_ref, analysis_ref, out_ref,
    table_ref, spectral_ref, rows_ref, send_ref, recv_ref, back_send_ref, back_recv_ref,
    wide_ref, sum_ref, right_ref, alpha_ref, beta_ref, gamma_ref,
    ratio_ref, inverse_ref, slope_ref, slopes_ref, edge_ref, edges_ref,
    table_sem, send_sem, recv_sem, back_send_sem, back_recv_sem, slope_send_sem, slope_recv_sem,
    edge_send_sem, edge_recv_sem,
):
    shells, ord_dev, _, degrees = field_ref.shape
    modes = 2 * ord_dev
    parts, rings = lax.axis_size("mode"), lax.axis_size("radial")
    me, ring = lax.axis_index("mode"), lax.axis_index("radial")
    mine = shells // parts
    count = 4 * shells
    width = table_ref.shape[3]
    lanes, blocks = width // 128, degrees // 128
    nr_total = shells * rings
    group = 2 if width < 256 and mine % 2 == 0 else 1

    def table_copy(chunk):
        return pltpu.make_async_copy(
            table_hbm.at[:, :, pl.ds(chunk * width, width)], table_ref.at[chunk], table_sem.at[chunk]
        )

    for chunk in range(chunks):
        table_copy(chunk).start()

    barrier = pltpu.get_barrier_semaphore()
    for hop in range(1, parts):
        pl.semaphore_signal(
            barrier, inc=1, device_id={"mode": lax.rem(me + hop, parts)},
            device_id_type=pl.DeviceIdType.MESH,
        )
    for hop in range(1, rings):
        pl.semaphore_signal(
            barrier, inc=1, device_id={"radial": lax.rem(ring + hop, rings)},
            device_id_type=pl.DeviceIdType.MESH,
        )

    def exchange(axis, hop, source, target, send, receive):
        here, size = (me, parts) if axis == "mode" else (ring, rings)
        return pltpu.make_async_remote_copy(
            src_ref=source, dst_ref=target, send_sem=send, recv_sem=receive,
            device_id={axis: lax.rem(here + hop, size)}, device_id_type=pl.DeviceIdType.MESH,
        )

    def lat_copy(chunk, hop, slot):
        to = lax.rem(me + hop, parts)
        return exchange(
            "mode", hop, send_ref.at[chunk, to], recv_ref.at[chunk, slot],
            send_sem.at[chunk, hop - 1], recv_sem.at[chunk, hop - 1],
        )

    def back_copy(chunk, hop, slot):
        to = lax.rem(me + hop, parts)
        return exchange(
            "mode", hop, back_send_ref.at[chunk, to], back_recv_ref.at[chunk, slot],
            back_send_sem.at[chunk, hop - 1], back_recv_sem.at[chunk, hop - 1],
        )

    def edge_copy(hop, slot):
        relayed = hop > 1 and hop % 2 == 1
        source = edges_ref.at[partner(ring, hop - 1, rings)] if relayed else edge_ref
        return pltpu.make_async_remote_copy(
            src_ref=source, dst_ref=edges_ref.at[slot],
            send_sem=edge_send_sem.at[hop - 1], recv_sem=edge_recv_sem.at[hop - 1],
            device_id={"radial": partner(ring, 1 if relayed else hop, rings)},
            device_id_type=pl.DeviceIdType.MESH,
        )

    def slope_copy(hop, slot):
        return exchange(
            "radial", hop, slope_ref, slopes_ref.at[slot],
            slope_send_sem.at[hop - 1], slope_recv_sem.at[hop - 1],
        )

    def stack(order, carry):
        spectral_ref[order] = jnp.concatenate(
            [ref[:, order, half, :] for half in range(2) for ref in (field_ref, flow_ref)], axis=0
        ).astype(jnp.bfloat16)
        return carry

    lax.fori_loop(0, ord_dev, stack, 0, unroll=2)

    for chunk in range(chunks):
        table_copy(chunk).wait()

        def transform(order, carry):
            lat = jnp.dot(
                spectral_ref[order], table_ref[chunk, order], preferred_element_type=jnp.float32
            )
            base = pl.multiple_of(order * count, count)
            for lane in range(lanes):
                rows_ref[lane, pl.ds(base, count), :] = lat[:, lane * 128 : (lane + 1) * 128]
            return carry

        lax.fori_loop(0, ord_dev, transform, 0, unroll=2)

        def pack(row, carry):
            which, shell = row // shells, row % shells
            part, local = shell // mine, shell % mine
            for lane in range(lanes):
                picked = rows_ref[lane, pl.ds(row, modes, stride=2 * shells), :]
                send_ref[chunk, part, which, local, :, lane * 128 : (lane + 1) * 128] = (
                    picked.astype(jnp.bfloat16)
                )
            return carry

        lax.fori_loop(0, 2 * shells, pack, 0, unroll=4)
        recv_ref[chunk, me] = send_ref[chunk, me]
        if chunk == 0:
            pl.semaphore_wait(barrier, parts + rings - 2)
        for hop in range(1, parts):
            lat_copy(chunk, hop, me).start()

    offset = nr_total * 7 // 13
    cut = [slice(block * 128, (block + 1) * 128) for block in range(blocks)]
    tile = (ord_dev, 128)
    blank = jnp.zeros(tile, jnp.float32)
    unity = jnp.ones(tile, jnp.float32)
    angulars = []
    for block in range(blocks):
        degree = (
            me * ord_dev
            + block * 128
            + lax.broadcasted_iota(jnp.int32, tile, 0)
            + lax.broadcasted_iota(jnp.int32, tile, 1)
        ).astype(jnp.float32)
        angulars.append(degree * (degree + 1.0))

    def factor(shell, carry):
        kappa = jnp.full(tile, kappa_ref[shell], jnp.float32)
        spot = jnp.full(tile, ring * shells + shell, jnp.int32)
        lower = jnp.where(spot > 0, -kappa, 0.0)
        upper = jnp.where(spot < nr_total - 1, -kappa, 0.0)
        radius = (offset + spot).astype(jnp.float32)
        weight = kappa / (radius * radius)
        new = []
        for block in range(blocks):
            ratio, pull = carry[block]
            diagonal = 1.0 + 2.0 * kappa + weight * angulars[block]
            inverse = 1.0 / (diagonal - lower * ratio)
            ratio = upper * inverse
            pull = -lower * pull * inverse
            inverse_ref[shell, :, cut[block]] = inverse
            ratio_ref[shell, :, cut[block]] = ratio
            beta_ref[shell, :, cut[block]] = pull
            new.append((ratio, pull))
        return tuple(new)

    outset = tuple((blank, unity) for _ in range(blocks))
    lax.fori_loop(0, shells, factor, outset)

    def unfactor(step, carry):
        shell = shells - 1 - step
        new = []
        for block in range(blocks):
            beta, gamma = carry[block]
            ratio = ratio_ref[shell, :, cut[block]]
            beta = beta_ref[shell, :, cut[block]] - ratio * beta
            gamma = -ratio * gamma
            beta_ref[shell, :, cut[block]] = beta
            gamma_ref[shell, :, cut[block]] = gamma
            new.append((beta, gamma))
        return tuple(new)

    lax.fori_loop(0, shells, unfactor, outset)
    for side, shell in enumerate((0, shells - 1)):
        slope_ref[2 * side] = beta_ref[shell]
        slope_ref[2 * side + 1] = gamma_ref[shell]
    slopes_ref[ring] = slope_ref[...]
    for hop in range(1, rings):
        slope_copy(hop, ring).start()

    for chunk in range(chunks):
        for hop in range(1, parts):
            lat_copy(chunk, hop, lax.rem(me + parts - hop, parts)).wait_recv()

        def multiply(step, carry):
            locals_ = [step * group + k for k in range(group)]
            grids = []
            for which in range(2):
                lat = jnp.concatenate(
                    [
                        jnp.concatenate(
                            [recv_ref[chunk, part, which, local] for part in range(parts)], axis=0
                        )
                        for local in locals_
                    ],
                    axis=1,
                )
                grids.append(jnp.dot(synth_ref[...], lat, preferred_element_type=jnp.float32))
            product = (grids[0] * grids[1]).astype(jnp.bfloat16)
            back = jnp.dot(analysis_ref[...], product, preferred_element_type=jnp.float32) * scale
            for k, local in enumerate(locals_):
                for part in range(parts):
                    back_send_ref[chunk, part, local] = back[
                        part * modes : (part + 1) * modes, k * width : (k + 1) * width
                    ].astype(jnp.bfloat16)
            return carry

        lax.fori_loop(0, mine // group, multiply, 0)
        back_recv_ref[chunk, me] = back_send_ref[chunk, me]
        for hop in range(1, parts):
            back_copy(chunk, hop, me).start()

    for chunk in range(chunks):
        for hop in range(1, parts):
            back_copy(chunk, hop, lax.rem(me + parts - hop, parts)).wait_recv()

        def widen(shell, carry):
            base = pl.multiple_of(shell * modes, modes)
            for lane in range(lanes):
                wide_ref[lane, pl.ds(base, modes), :] = back_recv_ref[
                    chunk, shell // mine, shell % mine, :, lane * 128 : (lane + 1) * 128
                ].astype(jnp.float32)
            return carry

        lax.fori_loop(0, shells, widen, 0, unroll=4)

        def untransform(order, carry):
            picked = jnp.concatenate(
                [
                    jnp.concatenate(
                        [
                            wide_ref[lane, pl.ds(2 * order + half, shells, stride=modes), :].astype(
                                jnp.bfloat16
                            )
                            for lane in range(lanes)
                        ],
                        axis=1,
                    )
                    for half in range(2)
                ],
                axis=0,
            )
            forcing = lax.dot_general(
                picked, table_ref[chunk, order], (((1,), (1,)), ((), ())),
                preferred_element_type=jnp.float32,
            )
            if chunk > 0:
                forcing = sum_ref[order] + forcing
            if chunk < chunks - 1:
                sum_ref[order] = forcing
                return carry
            for half in range(2):
                right = field_ref[:, order, half, :] + forcing[half * shells : (half + 1) * shells]
                for block in range(blocks):
                    right_ref[block, pl.ds(half * ord_dev + order, shells, stride=modes), :] = right[
                        :, block * 128 : (block + 1) * 128
                    ]
            return carry

        lax.fori_loop(0, ord_dev, untransform, 0, unroll=2)

    def forward(shell, carry):
        index = ring * shells + shell
        lower = jnp.where(jnp.full(tile, index, jnp.int32) > 0, -kappa_ref[shell], 0.0)
        start = pl.multiple_of(shell * modes, modes)
        new = []
        for block in range(blocks):
            inverse = inverse_ref[shell, :, cut[block]]
            value0 = (
                right_ref[block, pl.ds(start, ord_dev), :] - lower * carry[block][0]
            ) * inverse
            value1 = (
                right_ref[block, pl.ds(start + ord_dev, ord_dev), :] - lower * carry[block][1]
            ) * inverse
            alpha_ref[shell, :ord_dev, cut[block]] = value0
            alpha_ref[shell, ord_dev:, cut[block]] = value1
            new.append((value0, value1))
        return tuple(new)

    empty = tuple((blank, blank) for _ in range(blocks))
    lax.fori_loop(0, shells, forward, empty, unroll=4)

    def backward(step, carry):
        shell = shells - 1 - step
        new = []
        for block in range(blocks):
            ratio = ratio_ref[shell, :, cut[block]]
            alpha0 = alpha_ref[shell, :ord_dev, cut[block]] - ratio * carry[block][0]
            alpha1 = alpha_ref[shell, ord_dev:, cut[block]] - ratio * carry[block][1]
            alpha_ref[shell, :ord_dev, cut[block]] = alpha0
            alpha_ref[shell, ord_dev:, cut[block]] = alpha1
            new.append((alpha0, alpha1))
        return tuple(new)

    lax.fori_loop(0, shells, backward, empty, unroll=4)

    for side, shell in enumerate((0, shells - 1)):
        edge_ref[2 * side] = alpha_ref[shell, :ord_dev]
        edge_ref[2 * side + 1] = alpha_ref[shell, ord_dev:]
    edges_ref[ring] = edge_ref[...]
    direct = [hop for hop in range(1, rings) if hop == 1 or hop % 2 == 0]
    for hop in reversed(direct):
        edge_copy(hop, ring).start()
    for hop in range(1, rings):
        slope_copy(hop, lax.rem(ring + rings - hop, rings)).wait_recv()

    factors = []
    for block in range(blocks):
        slope, steps = blank, []
        for device in range(rings):
            head0, head1, tail0, tail1 = [slopes_ref[device, k, :, cut[block]] for k in range(4)]
            inverse = 1.0 / (1.0 - head0 * slope)
            gain = head1 * inverse
            steps.append((inverse, gain, slope))
            slope = tail1 + tail0 * slope * gain
        factors.append(steps)

    for hop in direct:
        edge_copy(hop, partner(ring, hop, rings)).wait_recv()
        if hop % 2 == 0:
            edge_copy(hop + 1, partner(ring, hop, rings)).start()
    for hop in range(3, rings, 2):
        edge_copy(hop, partner(ring, hop, rings)).wait_recv()

    spot = jnp.full(tile, ring, jnp.int32)
    for block in range(blocks):
        known = [blank, blank]
        lefts, firsts = [], []
        for device in range(rings):
            inverse, gain, slope = factors[block][device]
            head = slopes_ref[device, 0, :, cut[block]]
            tail = slopes_ref[device, 2, :, cut[block]]
            lefts.append((known, slope))
            const = [
                (edges_ref[device, c, :, cut[block]] + head * known[c]) * inverse for c in range(2)
            ]
            firsts.append((const, gain))
            known = [
                edges_ref[device, 2 + c, :, cut[block]] + tail * (known[c] + slope * const[c])
                for c in range(2)
            ]
        beyond, before, after = [blank, blank], [blank, blank], [blank, blank]
        for device in reversed(range(rings)):
            const, gain = firsts[device]
            left, tilt = lefts[device]
            here = spot == device
            start = [const[c] + gain * beyond[c] for c in range(2)]
            before = [jnp.where(here, left[c] + tilt * start[c], before[c]) for c in range(2)]
            after = [jnp.where(here, beyond[c], after[c]) for c in range(2)]
            beyond = start

        def emit(shell, carry):
            beta, gamma = beta_ref[shell, :, cut[block]], gamma_ref[shell, :, cut[block]]
            for half in range(2):
                out_ref[shell, :, half, cut[block]] = (
                    alpha_ref[shell, half * ord_dev : (half + 1) * ord_dev, cut[block]]
                    + beta * before[half]
                    + gamma * after[half]
                )
            return carry

        lax.fori_loop(0, shells, emit, 0, unroll=2)

    for chunk in range(chunks):
        for hop in range(1, parts):
            lat_copy(chunk, hop, me).wait_send()
            back_copy(chunk, hop, me).wait_send()
    for hop in range(1, rings):
        slope_copy(hop, ring).wait_send()
        edge_copy(hop, ring).wait_send()


def on_device(scalar_field, radial_flow, legendre, diffusivity):
    shells, ord_dev, _, degrees = scalar_field.shape
    lats = legendre.shape[2]
    parts, rings = lax.axis_size("mode"), lax.axis_size("radial")
    orders = ord_dev * parts
    modes = 2 * ord_dev
    mine = shells // parts
    assert rings & (rings - 1) == 0
    synth, analysis, scale = longitude_tables(orders)
    width = 128 if lats % 128 == 0 else lats
    chunks = lats // width
    lanes, blocks = width // 128, degrees // 128
    bf16, f32 = jnp.bfloat16, jnp.float32
    vmem = pl.BlockSpec(memory_space=pltpu.VMEM)
    dma = pltpu.SemaphoreType.DMA
    return pl.pallas_call(
        functools.partial(whole_step, chunks, scale),
        in_specs=[
            pl.BlockSpec(memory_space=pltpu.SMEM),
            pl.BlockSpec(memory_space=pl.ANY),
            vmem, vmem, vmem, vmem,
        ],
        out_specs=vmem,
        out_shape=jax.ShapeDtypeStruct(scalar_field.shape, f32),
        scratch_shapes=[
            pltpu.VMEM((chunks, ord_dev, degrees, width), bf16),
            pltpu.VMEM((ord_dev, 4 * shells, degrees), bf16),
            pltpu.VMEM((lanes, 4 * shells * ord_dev, 128), f32),
            pltpu.VMEM((chunks, parts, 2, mine, modes, width), bf16),
            pltpu.VMEM((chunks, parts, 2, mine, modes, width), bf16),
            pltpu.VMEM((chunks, parts, mine, modes, width), bf16),
            pltpu.VMEM((chunks, parts, mine, modes, width), bf16),
            pltpu.VMEM((lanes, shells * modes, 128), f32),
            pltpu.VMEM((ord_dev, 2 * shells, degrees), f32),
            pltpu.VMEM((blocks, shells * modes, 128), f32),
            pltpu.VMEM((shells, modes, degrees), f32),
            pltpu.VMEM((shells, ord_dev, degrees), f32),
            pltpu.VMEM((shells, ord_dev, degrees), f32),
            pltpu.VMEM((shells, ord_dev, degrees), f32),
            pltpu.VMEM((shells, ord_dev, degrees), f32),
            pltpu.VMEM((4, ord_dev, degrees), f32),
            pltpu.VMEM((rings, 4, ord_dev, degrees), f32),
            pltpu.VMEM((4, ord_dev, degrees), f32),
            pltpu.VMEM((rings, 4, ord_dev, degrees), f32),
            dma((chunks,)),
            dma((chunks, parts - 1)),
            dma((chunks, parts - 1)),
            dma((chunks, parts - 1)),
            dma((chunks, parts - 1)),
            dma((rings - 1,)),
            dma((rings - 1,)),
            dma((rings - 1,)),
            dma((rings - 1,)),
        ],
        compiler_params=params(collective_id=0, has_side_effects=True),
        name="whole_step",
    )(diffusivity, legendre, scalar_field, radial_flow, synth, analysis)


def solution(mesh):
    return jax.shard_map(
        on_device,
        mesh=mesh,
        in_specs=(
            P("radial", "mode", None, None),
            P("radial", "mode", None, None),
            P("mode", None, None),
            P("radial"),
        ),
        out_specs=P("radial", "mode", None, None),
        check_vma=False,
    )
```

```python
import functools
import math

import jax
import jax.numpy as jnp
import numpy as np
from jax import lax
from jax.experimental import pallas as pl
from jax.experimental.pallas import tpu as pltpu
from jax.sharding import PartitionSpec as P

NLON = 1536
VMEM_LIMIT = 60 * 1024 * 1024


def params(**more):
    return pltpu.CompilerParams(vmem_limit_bytes=VMEM_LIMIT, **more)


def grid_points(orders):
    needed = 3 * (orders - 1) + 1
    return next(q for q in range(128, NLON + 1, 128) if q >= needed and NLON % q == 0)


def longitude_tables(orders):
    points = grid_points(orders)
    stride = NLON // points
    phase = np.arange(orders)[:, None] * (np.arange(points) * stride)[None, :] % NLON
    angle = phase.astype(np.float32) * np.float32(2.0 * math.pi / NLON)
    paired = np.stack([np.cos(angle), -np.sin(angle)], axis=1).reshape(2 * orders, points)
    synth = (paired / np.float32(math.sqrt(orders))).astype(jnp.bfloat16)
    analysis = (paired * np.float32(math.sqrt(2.0 / NLON))).astype(jnp.bfloat16)
    return jnp.asarray(synth.T), jnp.asarray(analysis), float(stride)


def partner(here, hop, size):
    place, bit = 0, 1
    while bit < size:
        place = place + (here // bit + hop // bit) % 2 * bit
        bit *= 2
    return place


def whole_step(
    chunks, scale, kappa_ref, table_hbm, field_ref, flow_ref, synth_ref, analysis_ref, out_ref,
    table_ref, spectral_ref, rows_ref, send_ref, recv_ref, back_send_ref, back_recv_ref,
    wide_ref, sum_ref, right_ref, alpha_ref, beta_ref, gamma_ref,
    ratio_ref, inverse_ref, slope_ref, slopes_ref, edge_ref, edges_ref,
    table_sem, send_sem, recv_sem, back_send_sem, back_recv_sem, slope_send_sem, slope_recv_sem,
    edge_send_sem, edge_recv_sem,
):
    shells, ord_dev, _, degrees = field_ref.shape
    modes = 2 * ord_dev
    parts, rings = lax.axis_size("mode"), lax.axis_size("radial")
    me, ring = lax.axis_index("mode"), lax.axis_index("radial")
    mine = shells // parts
    count = 4 * shells
    width = table_ref.shape[3]
    lanes, blocks = width // 128, degrees // 128
    nr_total = shells * rings
    group = 2 if width < 256 and mine % 2 == 0 else 1

    def table_copy(chunk):
        return pltpu.make_async_copy(
            table_hbm.at[:, :, pl.ds(chunk * width, width)], table_ref.at[chunk], table_sem.at[chunk]
        )

    for chunk in range(chunks):
        table_copy(chunk).start()

    barrier = pltpu.get_barrier_semaphore()
    for hop in range(1, parts):
        pl.semaphore_signal(
            barrier, inc=1, device_id={"mode": lax.rem(me + hop, parts)},
            device_id_type=pl.DeviceIdType.MESH,
        )
    for hop in range(1, rings):
        pl.semaphore_signal(
            barrier, inc=1, device_id={"radial": lax.rem(ring + hop, rings)},
            device_id_type=pl.DeviceIdType.MESH,
        )

    def exchange(axis, hop, source, target, send, receive):
        here, size = (me, parts) if axis == "mode" else (ring, rings)
        return pltpu.make_async_remote_copy(
            src_ref=source, dst_ref=target, send_sem=send, recv_sem=receive,
            device_id={axis: lax.rem(here + hop, size)}, device_id_type=pl.DeviceIdType.MESH,
        )

    def lat_copy(chunk, hop, slot):
        to = lax.rem(me + hop, parts)
        return exchange(
            "mode", hop, send_ref.at[chunk, to], recv_ref.at[chunk, slot],
            send_sem.at[chunk, hop - 1], recv_sem.at[chunk, hop - 1],
        )

    def back_copy(chunk, hop, slot):
        to = lax.rem(me + hop, parts)
        return exchange(
            "mode", hop, back_send_ref.at[chunk, to], back_recv_ref.at[chunk, slot],
            back_send_sem.at[chunk, hop - 1], back_recv_sem.at[chunk, hop - 1],
        )

    def edge_copy(hop, slot):
        relayed = hop > 1 and hop % 2 == 1
        source = edges_ref.at[partner(ring, hop - 1, rings)] if relayed else edge_ref
        return pltpu.make_async_remote_copy(
            src_ref=source, dst_ref=edges_ref.at[slot],
            send_sem=edge_send_sem.at[hop - 1], recv_sem=edge_recv_sem.at[hop - 1],
            device_id={"radial": partner(ring, 1 if relayed else hop, rings)},
            device_id_type=pl.DeviceIdType.MESH,
        )

    def slope_copy(hop, slot):
        return exchange(
            "radial", hop, slope_ref, slopes_ref.at[slot],
            slope_send_sem.at[hop - 1], slope_recv_sem.at[hop - 1],
        )

    def stack(order, carry):
        spectral_ref[order] = jnp.concatenate(
            [ref[:, order, half, :] for half in range(2) for ref in (field_ref, flow_ref)], axis=0
        ).astype(jnp.bfloat16)
        return carry

    lax.fori_loop(0, ord_dev, stack, 0, unroll=4)

    for chunk in range(chunks):
        table_copy(chunk).wait()

        def transform(order, carry):
            lat = jnp.dot(
                spectral_ref[order], table_ref[chunk, order], preferred_element_type=jnp.float32
            )
            base = pl.multiple_of(order * count, count)
            for lane in range(lanes):
                rows_ref[lane, pl.ds(base, count), :] = lat[:, lane * 128 : (lane + 1) * 128]
            return carry

        lax.fori_loop(0, ord_dev, transform, 0, unroll=4)

        def pack(row, carry):
            which, shell = row // shells, row % shells
            part, local = shell // mine, shell % mine
            for lane in range(lanes):
                picked = rows_ref[lane, pl.ds(row, modes, stride=2 * shells), :]
                send_ref[chunk, part, which, local, :, lane * 128 : (lane + 1) * 128] = (
                    picked.astype(jnp.bfloat16)
                )
            return carry

        lax.fori_loop(0, 2 * shells, pack, 0, unroll=8)
        recv_ref[chunk, me] = send_ref[chunk, me]
        if chunk == 0:
            pl.semaphore_wait(barrier, parts + rings - 2)
        for hop in range(1, parts):
            lat_copy(chunk, hop, me).start()

    offset = nr_total * 7 // 13
    cut = [slice(block * 128, (block + 1) * 128) for block in range(blocks)]
    tile = (ord_dev, 128)
    blank = jnp.zeros(tile, jnp.float32)
    unity = jnp.ones(tile, jnp.float32)
    angulars = []
    for block in range(blocks):
        degree = (
            me * ord_dev
            + block * 128
            + lax.broadcasted_iota(jnp.int32, tile, 0)
            + lax.broadcasted_iota(jnp.int32, tile, 1)
        ).astype(jnp.float32)
        angulars.append(degree * (degree + 1.0))

    def factor(shell, carry):
        kappa = jnp.full(tile, kappa_ref[shell], jnp.float32)
        spot = jnp.full(tile, ring * shells + shell, jnp.int32)
        lower = jnp.where(spot > 0, -kappa, 0.0)
        upper = jnp.where(spot < nr_total - 1, -kappa, 0.0)
        radius = (offset + spot).astype(jnp.float32)
        weight = kappa / (radius * radius)
        new = []
        for block in range(blocks):
            ratio, pull = carry[block]
            diagonal = 1.0 + 2.0 * kappa + weight * angulars[block]
            inverse = 1.0 / (diagonal - lower * ratio)
            ratio = upper * inverse
            pull = -lower * pull * inverse
            inverse_ref[shell, :, cut[block]] = inverse
            ratio_ref[shell, :, cut[block]] = ratio
            beta_ref[shell, :, cut[block]] = pull
            new.append((ratio, pull))
        return tuple(new)

    outset = tuple((blank, unity) for _ in range(blocks))
    lax.fori_loop(0, shells, factor, outset)

    def unfactor(step, carry):
        shell = shells - 1 - step
        new = []
        for block in range(blocks):
            beta, gamma = carry[block]
            ratio = ratio_ref[shell, :, cut[block]]
            beta = beta_ref[shell, :, cut[block]] - ratio * beta
            gamma = -ratio * gamma
            beta_ref[shell, :, cut[block]] = beta
            gamma_ref[shell, :, cut[block]] = gamma
            new.append((beta, gamma))
        return tuple(new)

    lax.fori_loop(0, shells, unfactor, outset)
    for side, shell in enumerate((0, shells - 1)):
        slope_ref[2 * side] = beta_ref[shell]
        slope_ref[2 * side + 1] = gamma_ref[shell]
    slopes_ref[ring] = slope_ref[...]
    for hop in range(1, rings):
        slope_copy(hop, ring).start()

    for chunk in range(chunks):
        for hop in range(1, parts):
            lat_copy(chunk, hop, lax.rem(me + parts - hop, parts)).wait_recv()

        def multiply(step, carry):
            locals_ = [step * group + k for k in range(group)]
            grids = []
            for which in range(2):
                lat = jnp.concatenate(
                    [
                        jnp.concatenate(
                            [recv_ref[chunk, part, which, local] for part in range(parts)], axis=0
                        )
                        for local in locals_
                    ],
                    axis=1,
                )
                grids.append(jnp.dot(synth_ref[...], lat, preferred_element_type=jnp.float32))
            product = (grids[0] * grids[1]).astype(jnp.bfloat16)
            back = jnp.dot(analysis_ref[...], product, preferred_element_type=jnp.float32) * scale
            for k, local in enumerate(locals_):
                for part in range(parts):
                    back_send_ref[chunk, part, local] = back[
                        part * modes : (part + 1) * modes, k * width : (k + 1) * width
                    ].astype(jnp.bfloat16)
            return carry

        lax.fori_loop(0, mine // group, multiply, 0, unroll=2)
        back_recv_ref[chunk, me] = back_send_ref[chunk, me]
        for hop in range(1, parts):
            back_copy(chunk, hop, me).start()

    for chunk in range(chunks):
        for hop in range(1, parts):
            back_copy(chunk, hop, lax.rem(me + parts - hop, parts)).wait_recv()

        def widen(shell, carry):
            base = pl.multiple_of(shell * modes, modes)
            for lane in range(lanes):
                wide_ref[lane, pl.ds(base, modes), :] = back_recv_ref[
                    chunk, shell // mine, shell % mine, :, lane * 128 : (lane + 1) * 128
                ].astype(jnp.float32)
            return carry

        lax.fori_loop(0, shells, widen, 0, unroll=4)

        def untransform(order, carry):
            picked = jnp.concatenate(
                [
                    jnp.concatenate(
                        [
                            wide_ref[lane, pl.ds(2 * order + half, shells, stride=modes), :].astype(
                                jnp.bfloat16
                            )
                            for lane in range(lanes)
                        ],
                        axis=1,
                    )
                    for half in range(2)
                ],
                axis=0,
            )
            forcing = lax.dot_general(
                picked, table_ref[chunk, order], (((1,), (1,)), ((), ())),
                preferred_element_type=jnp.float32,
            )
            if chunk > 0:
                forcing = sum_ref[order] + forcing
            if chunk < chunks - 1:
                sum_ref[order] = forcing
                return carry
            for half in range(2):
                right = field_ref[:, order, half, :] + forcing[half * shells : (half + 1) * shells]
                for block in range(blocks):
                    right_ref[block, pl.ds(half * ord_dev + order, shells, stride=modes), :] = right[
                        :, block * 128 : (block + 1) * 128
                    ]
            return carry

        lax.fori_loop(0, ord_dev, untransform, 0, unroll=4)

    def forward(shell, carry):
        index = ring * shells + shell
        lower = jnp.where(jnp.full(tile, index, jnp.int32) > 0, -kappa_ref[shell], 0.0)
        start = pl.multiple_of(shell * modes, modes)
        new = []
        for block in range(blocks):
            inverse = inverse_ref[shell, :, cut[block]]
            value0 = (
                right_ref[block, pl.ds(start, ord_dev), :] - lower * carry[block][0]
            ) * inverse
            value1 = (
                right_ref[block, pl.ds(start + ord_dev, ord_dev), :] - lower * carry[block][1]
            ) * inverse
            alpha_ref[shell, :ord_dev, cut[block]] = value0
            alpha_ref[shell, ord_dev:, cut[block]] = value1
            new.append((value0, value1))
        return tuple(new)

    empty = tuple((blank, blank) for _ in range(blocks))
    lax.fori_loop(0, shells, forward, empty, unroll=4)

    def backward(step, carry):
        shell = shells - 1 - step
        new = []
        for block in range(blocks):
            ratio = ratio_ref[shell, :, cut[block]]
            alpha0 = alpha_ref[shell, :ord_dev, cut[block]] - ratio * carry[block][0]
            alpha1 = alpha_ref[shell, ord_dev:, cut[block]] - ratio * carry[block][1]
            alpha_ref[shell, :ord_dev, cut[block]] = alpha0
            alpha_ref[shell, ord_dev:, cut[block]] = alpha1
            new.append((alpha0, alpha1))
        return tuple(new)

    lax.fori_loop(0, shells, backward, empty, unroll=4)

    for side, shell in enumerate((0, shells - 1)):
        edge_ref[2 * side] = alpha_ref[shell, :ord_dev]
        edge_ref[2 * side + 1] = alpha_ref[shell, ord_dev:]
    edges_ref[ring] = edge_ref[...]
    direct = [hop for hop in range(1, rings) if hop == 1 or hop % 2 == 0]
    for hop in reversed(direct):
        edge_copy(hop, ring).start()
    for hop in range(1, rings):
        slope_copy(hop, lax.rem(ring + rings - hop, rings)).wait_recv()

    factors = []
    for block in range(blocks):
        slope, steps = blank, []
        for device in range(rings):
            head0, head1, tail0, tail1 = [slopes_ref[device, k, :, cut[block]] for k in range(4)]
            inverse = 1.0 / (1.0 - head0 * slope)
            gain = head1 * inverse
            steps.append((inverse, gain, slope))
            slope = tail1 + tail0 * slope * gain
        factors.append(steps)

    for hop in direct:
        edge_copy(hop, partner(ring, hop, rings)).wait_recv()
        if hop % 2 == 0:
            edge_copy(hop + 1, partner(ring, hop, rings)).start()
    for hop in range(3, rings, 2):
        edge_copy(hop, partner(ring, hop, rings)).wait_recv()

    spot = jnp.full(tile, ring, jnp.int32)
    for block in range(blocks):
        known = [blank, blank]
        lefts, firsts = [], []
        for device in range(rings):
            inverse, gain, slope = factors[block][device]
            head = slopes_ref[device, 0, :, cut[block]]
            tail = slopes_ref[device, 2, :, cut[block]]
            lefts.append((known, slope))
            const = [
                (edges_ref[device, c, :, cut[block]] + head * known[c]) * inverse for c in range(2)
            ]
            firsts.append((const, gain))
            known = [
                edges_ref[device, 2 + c, :, cut[block]] + tail * (known[c] + slope * const[c])
                for c in range(2)
            ]
        beyond, before, after = [blank, blank], [blank, blank], [blank, blank]
        for device in reversed(range(rings)):
            const, gain = firsts[device]
            left, tilt = lefts[device]
            here = spot == device
            start = [const[c] + gain * beyond[c] for c in range(2)]
            before = [jnp.where(here, left[c] + tilt * start[c], before[c]) for c in range(2)]
            after = [jnp.where(here, beyond[c], after[c]) for c in range(2)]
            beyond = start

        def emit(shell, carry):
            beta, gamma = beta_ref[shell, :, cut[block]], gamma_ref[shell, :, cut[block]]
            for half in range(2):
                out_ref[shell, :, half, cut[block]] = (
                    alpha_ref[shell, half * ord_dev : (half + 1) * ord_dev, cut[block]]
                    + beta * before[half]
                    + gamma * after[half]
                )
            return carry

        lax.fori_loop(0, shells, emit, 0, unroll=4)

    for chunk in range(chunks):
        for hop in range(1, parts):
            lat_copy(chunk, hop, me).wait_send()
            back_copy(chunk, hop, me).wait_send()
    for hop in range(1, rings):
        slope_copy(hop, ring).wait_send()
        edge_copy(hop, ring).wait_send()


def on_device(scalar_field, radial_flow, legendre, diffusivity):
    shells, ord_dev, _, degrees = scalar_field.shape
    lats = legendre.shape[2]
    parts, rings = lax.axis_size("mode"), lax.axis_size("radial")
    orders = ord_dev * parts
    modes = 2 * ord_dev
    mine = shells // parts
    assert rings & (rings - 1) == 0
    synth, analysis, scale = longitude_tables(orders)
    width = 128 if lats % 128 == 0 else lats
    chunks = lats // width
    lanes, blocks = width // 128, degrees // 128
    bf16, f32 = jnp.bfloat16, jnp.float32
    vmem = pl.BlockSpec(memory_space=pltpu.VMEM)
    dma = pltpu.SemaphoreType.DMA
    return pl.pallas_call(
        functools.partial(whole_step, chunks, scale),
        in_specs=[
            pl.BlockSpec(memory_space=pltpu.SMEM),
            pl.BlockSpec(memory_space=pl.ANY),
            vmem, vmem, vmem, vmem,
        ],
        out_specs=vmem,
        out_shape=jax.ShapeDtypeStruct(scalar_field.shape, f32),
        scratch_shapes=[
            pltpu.VMEM((chunks, ord_dev, degrees, width), bf16),
            pltpu.VMEM((ord_dev, 4 * shells, degrees), bf16),
            pltpu.VMEM((lanes, 4 * shells * ord_dev, 128), f32),
            pltpu.VMEM((chunks, parts, 2, mine, modes, width), bf16),
            pltpu.VMEM((chunks, parts, 2, mine, modes, width), bf16),
            pltpu.VMEM((chunks, parts, mine, modes, width), bf16),
            pltpu.VMEM((chunks, parts, mine, modes, width), bf16),
            pltpu.VMEM((lanes, shells * modes, 128), f32),
            pltpu.VMEM((ord_dev, 2 * shells, degrees), f32),
            pltpu.VMEM((blocks, shells * modes, 128), f32),
            pltpu.VMEM((shells, modes, degrees), f32),
            pltpu.VMEM((shells, ord_dev, degrees), f32),
            pltpu.VMEM((shells, ord_dev, degrees), f32),
            pltpu.VMEM((shells, ord_dev, degrees), f32),
            pltpu.VMEM((shells, ord_dev, degrees), f32),
            pltpu.VMEM((4, ord_dev, degrees), f32),
            pltpu.VMEM((rings, 4, ord_dev, degrees), f32),
            pltpu.VMEM((4, ord_dev, degrees), f32),
            pltpu.VMEM((rings, 4, ord_dev, degrees), f32),
            dma((chunks,)),
            dma((chunks, parts - 1)),
            dma((chunks, parts - 1)),
            dma((chunks, parts - 1)),
            dma((chunks, parts - 1)),
            dma((rings - 1,)),
            dma((rings - 1,)),
            dma((rings - 1,)),
            dma((rings - 1,)),
        ],
        compiler_params=params(collective_id=0, has_side_effects=True),
        name="whole_step",
    )(diffusivity, legendre, scalar_field, radial_flow, synth, analysis)


def solution(mesh):
    return jax.shard_map(
        on_device,
        mesh=mesh,
        in_specs=(
            P("radial", "mode", None, None),
            P("radial", "mode", None, None),
            P("mode", None, None),
            P("radial"),
        ),
        out_specs=P("radial", "mode", None, None),
        check_vma=False,
    )
```
